32 devices in a mesh: sec: 4 (over y, x), brick: 8 (over z, core).
Axes of the slice: x: 2, y: 2, z: 4, core: 2. Of those that a mesh axis runs over, the one named last changes fastest.
Arguments:
- velocity: float32 [3, 64, 256, 768], P(None, 'sec', 'brick'), may hold values from -10 to 10
- filter_taps: float32 [3, 9], replicated, may hold values from -2 to 2
- start_vectors: float32 [2, 32, 16], replicated, may hold values from -6 to 6
Outputs:
- basis_out: float32 [16, 9, 24576], P('sec', None, 'brick')
- energies: float32 [16, 16], P('sec')
The draws below stay inside these ranges and needn't reach their ends.
All inputs are finite; a program needn't handle non-finite values.
Results may differ from the reference program's by a relative error of at most 0.0029.
Values may be sent and summed in bfloat16 or wider, within the bound.
A program may use at most 64 MiB of HBM per device.

```python
import jax
import jax.numpy as jnp
from jax import lax

CY = 32
CZ = 24
MODES = 16
NS_STEPS = 8
NX = 256
SNAPS_ALL = 64
ROWS_ALL = 221184
N_SEC = 4


def draw_velocity(key, part):
    key_noise = jax.random.fold_in(key, 11)
    position = jnp.arange(NX, dtype=jnp.float32) / NX
    amplitude = (0.6 + 1.4 * position)[None, None, :, None]
    noise_field = jax.random.truncated_normal(key_noise, -4.0, 4.0, (3, SNAPS_ALL, NX, CY * CZ), jnp.float32)
    values = noise_field * amplitude
    return jnp.clip(values, -10.0, 10.0)


def centred(stream_key, shape, scale, bound, held_as=jnp.bfloat16):
    result = scale * jax.random.normal(stream_key, shape, jnp.float32)
    return jnp.clip(result, min=-bound, max=bound).astype(held_as)


def setup_inputs(seed: int = 0) -> dict:
    key_list = jax.random.split(jax.random.key(seed), 4)
    return {
        "velocity": draw_velocity(jax.random.fold_in(key_list[3], 71), 0),
        "filter_taps": centred(key_list[1], (3, 9), 9 ** -0.5, 2.0, jnp.float32),
        "start_vectors": centred(key_list[2], (2, 2 * MODES, MODES), 1.0, 6.0, jnp.float32),
    }


exact_mode = lax.Precision.HIGHEST
pair_list = ((0, 0), (0, 1), (0, 2), (1, 1), (1, 2), (2, 2))

def newton_root(matrix):
    eye_matrix = jnp.eye(matrix.shape[0], dtype=jnp.float32)
    scale_total = jnp.trace(matrix)
    current = matrix / scale_total
    inverse = eye_matrix
    for repeat in range(NS_STEPS):
        factor = 1.5 * eye_matrix - 0.5 * jnp.dot(inverse, current, precision=exact_mode)
        current = jnp.dot(current, factor, precision=exact_mode)
        inverse = jnp.dot(factor, inverse, precision=exact_mode)
    return (current * jnp.sqrt(scale_total), inverse / jnp.sqrt(scale_total))

def merge_basis(gram_matrix, start_basis):
    trace_total = jnp.trace(gram_matrix)
    subspace = start_basis
    for repeat in range(2):
        image_block = jnp.dot(gram_matrix, subspace, precision=exact_mode) / trace_total
        inverse_root = newton_root(jnp.dot(image_block.T, image_block, precision=exact_mode))[1]
        subspace = jnp.dot(image_block, inverse_root, precision=exact_mode)
    metric = jnp.dot(subspace.T, jnp.dot(gram_matrix, subspace, precision=exact_mode), precision=exact_mode) / trace_total
    project = jnp.dot(subspace, newton_root(metric)[1], precision=exact_mode)
    gram_project = jnp.dot(gram_matrix, project, precision=exact_mode)
    covariance = jnp.dot(gram_project.T, gram_project, precision=exact_mode) / trace_total
    coeffs = jnp.dot(project, newton_root(covariance)[0], precision=exact_mode) / jnp.sqrt(trace_total)
    return (coeffs, covariance)

def wrap_matrix(kernel_taps, extent):
    cell_index = jnp.arange(extent)[:, None]
    out_index = jnp.arange(extent // 2)[None, :]
    matrix = jnp.zeros((extent, extent // 2), jnp.float32)
    for offset in range(9):
        matrix = matrix + kernel_taps[offset] * (cell_index == (2 * out_index + offset - 4) % extent).astype(jnp.float32)
    return matrix

def section_snapshots(velocity_part, filter_taps):
    along_y = wrap_matrix(filter_taps[1], CY)
    along_z = wrap_matrix(filter_taps[2], CZ)
    shaped = velocity_part.reshape(3, MODES, NX, CY, CZ)
    pieces = []
    for number in range(9):
        if number < 3:
            values = shaped[number]
        else:
            index_one, index_two = pair_list[number - 3]
            values = shaped[index_one] * shaped[index_two]
        filtered = jnp.einsum('sxyz,zk->sxyk', values, along_z, precision=exact_mode)
        filtered = jnp.einsum('sxyk,yj->sxjk', filtered, along_y, precision=exact_mode)
        padded = jnp.concatenate([filtered[:, NX - 4:], filtered, filtered[:, :4]], axis=1)
        summed = jnp.zeros((MODES, NX // 2, CY // 2, CZ // 2), jnp.float32)
        for offset in range(9):
            summed = summed + filter_taps[0, offset] * padded[:, offset:offset + NX - 1:2]
        pieces.append(summed.reshape(MODES, NX // 2 * (CY // 2) * (CZ // 2)))
    return jnp.stack(pieces, axis=1).astype(jnp.bfloat16).reshape(MODES, ROWS_ALL)

def reference(velocity, filter_taps, start_vectors):
    sections = [section_snapshots(velocity[:, number * MODES:(number + 1) * MODES], filter_taps) for number in range(N_SEC)]
    level_rows = []
    for pair_index in range(2):
        stacked = jnp.concatenate([sections[2 * pair_index], sections[2 * pair_index + 1]], axis=0)
        gram_pair = jnp.dot(stacked, stacked.T, preferred_element_type=jnp.float32)
        coeffs = merge_basis(gram_pair, start_vectors[0])[0]
        level_rows.append(jnp.dot(coeffs.T, stacked, precision=exact_mode, preferred_element_type=jnp.float32))
    stacked_top = jnp.concatenate(level_rows, axis=0)
    gram_top = jnp.dot(stacked_top, stacked_top.T, precision=exact_mode)
    coeffs_top, covariance = merge_basis(gram_top, start_vectors[1])
    basis_out = jnp.dot(coeffs_top.T, stacked_top, precision=exact_mode)
    energies = covariance / (SNAPS_ALL * ROWS_ALL)
    return (basis_out.reshape(MODES, 9, ROWS_ALL // 9), energies)
```

```python
import functools

import jax
import jax.numpy as jnp
from jax import lax
from jax.experimental import pallas as pl
from jax.experimental.pallas import tpu as pltpu
from jax.sharding import PartitionSpec as P

CY = 32
CZ = 24
NS_STEPS = 8
TAPS = 9
FIELDS = 9
LAG = 1
GROUP = 3
MESH = pl.DeviceIdType.MESH
F32 = jnp.float32
BF16 = jnp.bfloat16


def exact(a, b, dims=((1,), (0,))):
    return lax.dot_general(
        a, b, (dims, ((), ())), precision=lax.Precision.HIGHEST, preferred_element_type=F32
    )


def fast(a, b, dims=((1,), (0,))):
    return lax.dot_general(a, b, (dims, ((), ())), preferred_element_type=F32)


def split(value):
    high = value.astype(BF16)
    return high, (value - high.astype(F32)).astype(BF16)


def grid_of(shape, dim):
    return lax.broadcasted_iota(jnp.int32, shape, dim).astype(F32)


def eye_of(size):
    shape = (size, size)
    return (
        lax.broadcasted_iota(jnp.int32, shape, 0) == lax.broadcasted_iota(jnp.int32, shape, 1)
    ).astype(F32)


def trace_of(matrix):
    return jnp.sum(matrix * eye_of(matrix.shape[0]), keepdims=True)


def pick_taps(taps_ref, dim, offset):
    total = jnp.zeros_like(offset)
    for tap in range(TAPS):
        total = jnp.where(offset == float(tap), taps_ref[dim, tap], total)
    return total


def newton_root(matrices, square):
    eye_matrix = eye_of(matrices[0].shape[0])
    scales = [trace_of(m) for m in matrices]
    current = [m / s for m, s in zip(matrices, scales)]
    inverse = [eye_matrix for _ in matrices]
    for step in range(NS_STEPS):
        if step == 0:
            factor = [1.5 * eye_matrix - 0.5 * y for y in current]
        else:
            factor = [1.5 * eye_matrix - 0.5 * exact(z, y) for z, y in zip(inverse, current)]
        last = step == NS_STEPS - 1
        if square or not last:
            current = [exact(y, e) for y, e in zip(current, factor)]
        if step == 0:
            inverse = factor
        elif not (square and last):
            inverse = [exact(e, z) for z, e in zip(inverse, factor)]
    if square:
        return [y * jnp.sqrt(s) for y, s in zip(current, scales)]
    return [z / jnp.sqrt(s) for z, s in zip(inverse, scales)]


def merge_bases(grams, start):
    traces = [trace_of(g) for g in grams]
    basis = [start for _ in grams]
    for repeat in range(2):
        image = [exact(g, q) / t for g, q, t in zip(grams, basis, traces)]
        roots = newton_root([exact(b, b, ((0,), (0,))) for b in image], False)
        basis = [exact(b, r) for b, r in zip(image, roots)]
    image = [exact(g, q) for g, q in zip(grams, basis)]
    metric = [exact(q, b, ((0,), (0,))) / t for q, b, t in zip(basis, image, traces)]
    roots = newton_root(metric, False)
    project = [exact(q, r) for q, r in zip(basis, roots)]
    image = [exact(b, r) for b, r in zip(image, roots)]
    covariance = [exact(b, b, ((0,), (0,))) / t for b, t in zip(image, traces)]
    roots = newton_root(covariance, True)
    coeffs = [exact(p, r) / jnp.sqrt(t) for p, r, t in zip(project, roots, traces)]
    return coeffs, covariance


def kernel(
    n_sec, n_brick, total_values,
    velocity_ref, taps_ref, start_ref,
    out_ref, energy_ref,
    field_ref, cross_ref, rows_ref, edge_ref, halo_out, halo_in, own_ref, all_ref,
    gram_out, gram_in, brick_out, brick_in, piece_ref, sent_ref, land_ref,
    load_sem, halo_send, halo_recv, part_send, part_recv,
    gram_send, gram_recv, brick_send, brick_recv, out_send, out_recv,
):
    snaps, rows = velocity_ref.shape[1], velocity_ref.shape[2]
    cells = velocity_ref.shape[3]
    reduced = cells // 4
    groups = rows // 4 + 2
    batch = rows_ref.shape[0] // (2 * groups)
    share = snaps // n_sec
    held = own_ref.shape[1] // n_sec
    me = lax.axis_index("sec")
    brick = lax.axis_index("brick")
    low = lax.rem(brick + n_brick - 1, n_brick)
    high = lax.rem(brick + 1, n_brick)
    bits = n_brick.bit_length() - 1
    flips = []
    for bit in range(bits):
        mask = 2**bit
        flips.append(brick + mask - 2 * mask * lax.rem(brick // mask, 2))

    loads = []
    for number in range(3):
        copy = pltpu.make_async_copy(
            velocity_ref.at[number], field_ref.at[number], load_sem.at[number]
        )
        copy.start()
        loads.append(copy)

    barrier = pltpu.get_barrier_semaphore()
    for target in [low, high] + flips:
        pl.semaphore_signal(barrier, inc=1, device_id=(me, target), device_id_type=MESH)
    for step in range(1, n_sec):
        pl.semaphore_signal(
            barrier, inc=1, device_id=(lax.rem(me + step, n_sec), brick), device_id_type=MESH
        )

    shape = (cells, reduced)
    cell, point = grid_of(shape, 0), grid_of(shape, 1)
    y = jnp.floor((cell + 0.5) * (1.0 / CZ))
    z = cell - y * CZ
    j = jnp.floor((point + 0.5) * (2.0 / CZ))
    k = point - j * (CZ // 2)
    off_y = y - 2.0 * j + 4.0
    off_y = jnp.where(off_y < 0.0, off_y + CY, off_y)
    off_y = jnp.where(off_y >= CY, off_y - CY, off_y)
    off_z = z - 2.0 * k + 4.0
    off_z = jnp.where(off_z < 0.0, off_z + CZ, off_z)
    off_z = jnp.where(off_z >= CZ, off_z - CZ, off_z)
    upper, lower = split(pick_taps(taps_ref, 1, off_y) * pick_taps(taps_ref, 2, off_z))
    cross_ref[0:cells, :] = upper
    cross_ref[cells : 2 * cells, :] = upper
    cross_ref[2 * cells :, :] = lower

    shape = (2 * groups * batch, batch * rows)
    target, source = grid_of(shape, 0), grid_of(shape, 1)
    parity = (target >= groups * batch).astype(F32)
    rest = target - parity * (groups * batch)
    pair = jnp.floor((rest + 0.5) * (1.0 / batch))
    snap = rest - pair * batch
    snap_in = jnp.floor((source + 0.5) * (1.0 / rows))
    offset = (source - snap_in * rows) - 2.0 * (2.0 * pair + parity - 2.0) + 4.0
    offset = jnp.where(snap == snap_in, offset, -1.0)
    upper, lower = split(pick_taps(taps_ref, 0, offset))
    width = batch * rows
    rows_ref[:, 0:width] = upper
    rows_ref[:, width : 2 * width] = upper
    rows_ref[:, 2 * width :] = lower

    def halo_copy(field, side):
        return pltpu.make_async_remote_copy(
            src_ref=halo_out.at[field, side],
            dst_ref=halo_in.at[field, 1 - side],
            send_sem=halo_send.at[field, side],
            recv_sem=halo_recv.at[field, 1 - side],
            device_id=(me, low if side == 0 else high),
            device_id_type=MESH,
        )

    def part_copy(field, step):
        target = lax.rem(me + step, n_sec)
        return pltpu.make_async_remote_copy(
            src_ref=own_ref.at[field, pl.ds(target * held, held)],
            dst_ref=all_ref.at[field, :, me],
            send_sem=part_send.at[field, step - 1],
            recv_sem=part_recv.at[field, step - 1],
            device_id=(target, brick),
            device_id_type=MESH,
        )

    def inside(step):
        target = lax.rem(me + step, n_sec)
        return (target > 0) & (target < n_sec - 1)

    def filtered(fields, values):
        inner = []
        for value in values:
            upper, lower = split(value.reshape(snaps * rows, cells))
            inner.append(fast(jnp.concatenate([upper, lower, upper], axis=1), cross_ref[...]))
        half = groups * batch
        results = []
        for value in inner:
            upper, lower = split(value)
            blocks = []
            for start in range(0, snaps * rows, width):
                high_part, low_part = upper[start : start + width], lower[start : start + width]
                outer = fast(rows_ref[...], jnp.concatenate([high_part, low_part, high_part], axis=0))
                joined = jnp.concatenate([outer[:half], outer[half:]], axis=1)
                blocks.append(joined.reshape(groups, batch, 2 * reduced))
            results.append(jnp.concatenate(blocks, axis=1))
        if fields[0] == 0:
            pl.semaphore_wait(barrier, 2 + bits + n_sec - 1)
        for field, joined in zip(fields, results):
            halo_out[field, 0] = joined[0].astype(BF16)
            halo_out[field, 1] = joined[groups - 1].astype(BF16)
            edge_ref[field, 0] = joined[1]
            edge_ref[field, 1] = joined[groups - 2]
            own_ref[field, pl.ds(1, groups - 4)] = joined[2 : groups - 2].astype(BF16)
            halo_copy(field, 0).start()
            halo_copy(field, 1).start()
            for step in range(1, n_sec):
                @pl.when(inside(step))
                def _():
                    part_copy(field, step).start()

    def finish(field):
        halo_copy(field, 1).wait_recv()
        own_ref[field, 0] = (edge_ref[field, 0] + halo_in[field, 0].astype(F32)).astype(BF16)
        halo_copy(field, 0).wait_recv()
        own_ref[field, groups - 3] = (edge_ref[field, 1] + halo_in[field, 1].astype(F32)).astype(BF16)
        for step in range(1, n_sec):
            @pl.when(jnp.logical_not(inside(step)))
            def _():
                part_copy(field, step).start()
        for piece in range(held):
            all_ref[field, piece, me] = own_ref[field, me * held + piece]

    for copy in loads:
        copy.wait()

    def source(field):
        if field < 3:
            return field_ref[field]
        number = field - 3
        one = number // 3 + number // 5
        two = number - 3 * one + one * (one - 1) // 2 + one
        return field_ref[one] * field_ref[two]

    done = 0
    for first in range(0, FIELDS, GROUP):
        fields = list(range(first, min(first + GROUP, FIELDS)))
        filtered(fields, [source(field) for field in fields])
        while done + LAG <= first:
            finish(done)
            done += 1
    for field in range(done, FIELDS):
        finish(field)

    count = n_sec * snaps
    gram = jnp.zeros((count, count), F32)
    for field in range(FIELDS):
        for step in range(1, n_sec):
            part_copy(field, step).wait_recv()
        for piece in range(held):
            block = all_ref[field, piece].reshape(count, 2 * reduced)
            gram = gram + fast(block, block, ((1,), (1,)))

    half = count // 2
    gram_out[...] = jnp.concatenate([gram[:half], gram[half:]], axis=1)
    gram_in[me] = gram_out[...]
    copies = []
    for step in range(1, n_sec):
        copy = pltpu.make_async_remote_copy(
            src_ref=gram_out,
            dst_ref=gram_in.at[me],
            send_sem=gram_send.at[step - 1],
            recv_sem=gram_recv.at[step - 1],
            device_id=(lax.rem(me + step, n_sec), brick),
            device_id_type=MESH,
        )
        copy.start()
        copies.append(copy)
    for copy in copies:
        copy.wait_recv()
    total = gram_in[0]
    for step in range(1, n_sec):
        total = total + gram_in[step]
    for bit in range(bits):
        brick_out[bit] = total
        copy = pltpu.make_async_remote_copy(
            src_ref=brick_out.at[bit],
            dst_ref=brick_in.at[bit],
            send_sem=brick_send.at[bit],
            recv_sem=brick_recv.at[bit],
            device_id=(me, flips[bit]),
            device_id_type=MESH,
        )
        copy.start()
        copies.append(copy)
        copy.wait_recv()
        total = total + brick_in[bit]
    gram = jnp.concatenate([total[:, :count], total[:, count:]], axis=0)

    half = count // 2
    lower_bases, _ = merge_bases([gram[:half, :half], gram[half:, half:]], start_ref[0].T)
    blank = jnp.zeros_like(lower_bases[0])
    blocks = jnp.concatenate(
        [
            jnp.concatenate([lower_bases[0], blank], axis=1),
            jnp.concatenate([blank, lower_bases[1]], axis=1),
        ],
        axis=0,
    )
    top = exact(blocks, exact(gram, blocks), ((0,), (0,)))
    (coeffs,), (covariance,) = merge_bases([top], start_ref[1].T)
    weights = exact(coeffs, blocks, ((0,), (1,)))
    upper, lower = split(weights)
    weights = jnp.concatenate([upper, lower], axis=0)
    shape = (share, snaps)
    pick = (
        lax.broadcasted_iota(jnp.int32, shape, 1)
        == lax.broadcasted_iota(jnp.int32, shape, 0) + me * share
    ).astype(F32)
    energy_ref[...] = exact(pick, covariance) / total_values

    outs = []
    for piece in range(held):
        for field in range(FIELDS):
            block = all_ref[field, piece].reshape(count, 2 * reduced)
            values = fast(weights, block)
            piece_ref[:, field, :] = values[:snaps] + values[snaps:]
        sent_ref[piece] = piece_ref[...].astype(BF16)
        for step in range(1, n_sec):
            target = lax.rem(me + step, n_sec)
            copy = pltpu.make_async_remote_copy(
                src_ref=sent_ref.at[piece, pl.ds(target * share, share)],
                dst_ref=land_ref.at[piece, step - 1],
                send_sem=out_send.at[piece, step - 1],
                recv_sem=out_recv.at[piece, step - 1],
                device_id=(target, brick),
                device_id_type=MESH,
            )
            copy.start()
            outs.append((piece, step, copy))
        place = pl.ds(pl.multiple_of((me * held + piece) * 2 * reduced, 2 * reduced), 2 * reduced)
        out_ref[:, :, place] = piece_ref[pl.ds(me * share, share)]

    @pl.loop(0, FIELDS)
    def _(field):
        for side in range(2):
            halo_copy(field, side).wait_send()
        for step in range(1, n_sec):
            part_copy(field, step).wait_send()

    for copy in copies:
        copy.wait_send()
    for piece, step, copy in outs:
        copy.wait_recv()
        source = lax.rem(me + n_sec - step, n_sec)
        place = pl.ds(
            pl.multiple_of((source * held + piece) * 2 * reduced, 2 * reduced), 2 * reduced
        )
        out_ref[:, :, place] = land_ref[piece, step - 1].astype(F32)
    for _, _, copy in outs:
        copy.wait_send()


def per_device(n_sec, n_brick, velocity, filter_taps, start_vectors):
    _, snaps, rows, cells = velocity.shape
    reduced = cells // 4
    groups = rows // 4 + 2
    share = snaps // n_sec
    held = rows // 4 // n_sec
    bits = max(n_brick.bit_length() - 1, 1)
    count = n_sec * snaps
    batch = max(1, min(snaps, 256 // rows))
    total_values = n_sec * snaps * FIELDS * (rows // 2) * reduced * n_brick
    width = 2 * reduced
    dma = pltpu.SemaphoreType.DMA
    return pl.pallas_call(
        functools.partial(kernel, n_sec, n_brick, total_values),
        out_shape=(
            jax.ShapeDtypeStruct((share, FIELDS, rows // 2 * reduced), F32),
            jax.ShapeDtypeStruct((share, snaps), F32),
        ),
        in_specs=[
            pl.BlockSpec(memory_space=pl.ANY),
            pl.BlockSpec(memory_space=pltpu.SMEM),
            pl.BlockSpec(memory_space=pltpu.VMEM),
        ],
        out_specs=(
            pl.BlockSpec(memory_space=pltpu.VMEM),
            pl.BlockSpec(memory_space=pltpu.VMEM),
        ),
        scratch_shapes=[
            pltpu.VMEM((3, snaps, rows, cells), F32),
            pltpu.VMEM((3 * cells, reduced), BF16),
            pltpu.VMEM((2 * groups * batch, 3 * batch * rows), BF16),
            pltpu.VMEM((FIELDS, 2, snaps, width), F32),
            pltpu.VMEM((FIELDS, 2, snaps, width), BF16),
            pltpu.VMEM((FIELDS, 2, snaps, width), BF16),
            pltpu.VMEM((FIELDS, groups - 2, snaps, width), BF16),
            pltpu.VMEM((FIELDS, held, n_sec, snaps, width), BF16),
            pltpu.VMEM((count // 2, 2 * count), F32),
            pltpu.VMEM((n_sec, count // 2, 2 * count), F32),
            pltpu.VMEM((bits, count // 2, 2 * count), F32),
            pltpu.VMEM((bits, count // 2, 2 * count), F32),
            pltpu.VMEM((snaps, FIELDS, width), F32),
            pltpu.VMEM((held, snaps, FIELDS, width), BF16),
            pltpu.VMEM((held, n_sec - 1, share, FIELDS, width), BF16),
            dma((3,)),
            dma((FIELDS, 2)),
            dma((FIELDS, 2)),
            dma((FIELDS, n_sec - 1)),
            dma((FIELDS, n_sec - 1)),
            dma((n_sec - 1,)),
            dma((n_sec - 1,)),
            dma((bits,)),
            dma((bits,)),
            dma((held, n_sec - 1)),
            dma((held, n_sec - 1)),
        ],
        compiler_params=pltpu.CompilerParams(
            collective_id=0, has_side_effects=True, vmem_limit_bytes=60 * 1024 * 1024
        ),
    )(velocity, filter_taps, jnp.transpose(start_vectors, (0, 2, 1)))


def solution(mesh):
    in_specs = (P(None, "sec", "brick", None), P(), P())
    out_specs = (P("sec", None, "brick"), P("sec", None))
    return jax.shard_map(
        functools.partial(per_device, mesh.shape["sec"], mesh.shape["brick"]),
        mesh=mesh, in_specs=in_specs, out_specs=out_specs, check_vma=False,
    )
```

```python
import functools

import jax
import jax.numpy as jnp
from jax import lax
from jax.experimental import pallas as pl
from jax.experimental.pallas import tpu as pltpu
from jax.sharding import PartitionSpec as P

CY = 32
CZ = 24
NS_STEPS = 8
TAPS = 9
FIELDS = 9
GROUP = 3
MESH = pl.DeviceIdType.MESH
F32 = jnp.float32
BF16 = jnp.bfloat16


def exact(a, b, dims=((1,), (0,))):
    return lax.dot_general(
        a, b, (dims, ((), ())), precision=lax.Precision.HIGHEST, preferred_element_type=F32
    )


def fast(a, b, dims=((1,), (0,))):
    return lax.dot_general(a, b, (dims, ((), ())), preferred_element_type=F32)


def split(value):
    high = value.astype(BF16)
    return high, (value - high.astype(F32)).astype(BF16)


def grid_of(shape, dim):
    return lax.broadcasted_iota(jnp.int32, shape, dim).astype(F32)


def eye_of(size):
    shape = (size, size)
    return (
        lax.broadcasted_iota(jnp.int32, shape, 0) == lax.broadcasted_iota(jnp.int32, shape, 1)
    ).astype(F32)


def trace_of(matrix):
    return jnp.sum(matrix * eye_of(matrix.shape[0]), keepdims=True)


def pick_taps(taps_ref, dim, offset):
    total = jnp.zeros_like(offset)
    for tap in range(TAPS):
        total = jnp.where(offset == float(tap), taps_ref[dim, tap], total)
    return total


def radices(size):
    result, stride = [], 1
    while size > 1:
        radix = 4 if size % 4 == 0 else 2
        result.append((stride, radix))
        stride, size = stride * radix, size // radix
    return result


def newton_root(matrices, square):
    eye_matrix = eye_of(matrices[0].shape[0])
    scales = [trace_of(m) for m in matrices]
    current = [m / s for m, s in zip(matrices, scales)]
    inverse = [eye_matrix for _ in matrices]
    for step in range(NS_STEPS):
        if step == 0:
            factor = [1.5 * eye_matrix - 0.5 * y for y in current]
        else:
            factor = [1.5 * eye_matrix - 0.5 * exact(z, y) for z, y in zip(inverse, current)]
        last = step == NS_STEPS - 1
        if square or not last:
            current = [exact(y, e) for y, e in zip(current, factor)]
        if step == 0:
            inverse = factor
        elif not (square and last):
            inverse = [exact(e, z) for z, e in zip(inverse, factor)]
    if square:
        return [y * jnp.sqrt(s) for y, s in zip(current, scales)]
    return [z / jnp.sqrt(s) for z, s in zip(inverse, scales)]


def merge_bases(grams, start):
    traces = [trace_of(g) for g in grams]
    basis = [start for _ in grams]
    for repeat in range(2):
        image = [exact(g, q) / t for g, q, t in zip(grams, basis, traces)]
        roots = newton_root([exact(b, b, ((0,), (0,))) for b in image], False)
        basis = [exact(b, r) for b, r in zip(image, roots)]
    image = [exact(g, q) for g, q in zip(grams, basis)]
    metric = [exact(q, b, ((0,), (0,))) / t for q, b, t in zip(basis, image, traces)]
    roots = newton_root(metric, False)
    project = [exact(q, r) for q, r in zip(basis, roots)]
    image = [exact(b, r) for b, r in zip(image, roots)]
    covariance = [exact(b, b, ((0,), (0,))) / t for b, t in zip(image, traces)]
    roots = newton_root(covariance, True)
    coeffs = [exact(p, r) / jnp.sqrt(t) for p, r, t in zip(project, roots, traces)]
    return coeffs, covariance


def kernel(
    n_sec, n_brick, total_values,
    velocity_ref, taps_ref, start_ref,
    out_ref, energy_ref,
    field_ref, cross_ref, rows_ref, edge_ref, halo_out, halo_in, own_ref, all_ref,
    gram_out, core_in, z_in, sec_in, total_ref, piece_ref, sent_ref, land_ref,
    load_sem, halo_send, halo_recv, part_send, part_recv,
    core_send, core_recv, z_send, z_recv, sec_send, sec_recv, out_send, out_recv,
):
    snaps, rows = velocity_ref.shape[1], velocity_ref.shape[2]
    cells = velocity_ref.shape[3]
    reduced = cells // 4
    groups = rows // 4 + 2
    batch = rows_ref.shape[0] // (2 * groups)
    share = snaps // n_sec
    held = own_ref.shape[1]
    me = lax.axis_index("sec")
    brick = lax.axis_index("brick")
    low = lax.rem(brick + n_brick - 1, n_brick)
    high = lax.rem(brick + 1, n_brick)
    core = lax.rem(brick, 2)
    partner = brick + 1 - 2 * core
    stages = []
    for stride, radix in radices(n_brick // 2):
        digit = lax.rem(brick // (2 * stride), radix)
        peers = [
            brick + 2 * stride * (lax.rem(digit + step, radix) - digit) for step in range(1, radix)
        ]
        stages.append((digit, peers))
    near = [low, high] + [peer for _, peers in stages for peer in peers]

    loads = []
    for number in range(3):
        copy = pltpu.make_async_copy(
            velocity_ref.at[number], field_ref.at[number], load_sem.at[number]
        )
        copy.start()
        loads.append(copy)

    barrier = pltpu.get_barrier_semaphore()
    for target in near:
        pl.semaphore_signal(barrier, inc=1, device_id=(me, target), device_id_type=MESH)
    for step in range(1, n_sec):
        pl.semaphore_signal(
            barrier, inc=1, device_id=(lax.rem(me + step, n_sec), brick), device_id_type=MESH
        )

    shape = (cells, reduced)
    cell, point = grid_of(shape, 0), grid_of(shape, 1)
    y = jnp.floor((cell + 0.5) * (1.0 / CZ))
    z = cell - y * CZ
    j = jnp.floor((point + 0.5) * (2.0 / CZ))
    k = point - j * (CZ // 2)
    off_y = y - 2.0 * j + 4.0
    off_y = jnp.where(off_y < 0.0, off_y + CY, off_y)
    off_y = jnp.where(off_y >= CY, off_y - CY, off_y)
    off_z = z - 2.0 * k + 4.0
    off_z = jnp.where(off_z < 0.0, off_z + CZ, off_z)
    off_z = jnp.where(off_z >= CZ, off_z - CZ, off_z)
    upper, lower = split(pick_taps(taps_ref, 1, off_y) * pick_taps(taps_ref, 2, off_z))
    cross_ref[0:cells, :] = upper
    cross_ref[cells : 2 * cells, :] = upper
    cross_ref[2 * cells :, :] = lower

    shape = (2 * groups * batch, batch * rows)
    target, source = grid_of(shape, 0), grid_of(shape, 1)
    parity = (target >= groups * batch).astype(F32)
    rest = target - parity * (groups * batch)
    pair = jnp.floor((rest + 0.5) * (1.0 / batch))
    snap = rest - pair * batch
    snap_in = jnp.floor((source + 0.5) * (1.0 / rows))
    offset = (source - snap_in * rows) - 2.0 * (2.0 * pair + parity - 2.0) + 4.0
    offset = jnp.where(snap == snap_in, offset, -1.0)
    upper, lower = split(pick_taps(taps_ref, 0, offset))
    width = batch * rows
    rows_ref[:, 0:width] = upper
    rows_ref[:, width : 2 * width] = upper
    rows_ref[:, 2 * width :] = lower

    def halo_copy(number, side):
        fields = pl.ds(number * GROUP, GROUP)
        return pltpu.make_async_remote_copy(
            src_ref=halo_out.at[side, fields],
            dst_ref=halo_in.at[1 - side, fields],
            send_sem=halo_send.at[number, side],
            recv_sem=halo_recv.at[number, 1 - side],
            device_id=(me, low if side == 0 else high),
            device_id_type=MESH,
        )

    def part_copy(number, step, first, size):
        fields = pl.ds(number * GROUP, GROUP)
        target = lax.rem(me + step, n_sec)
        return pltpu.make_async_remote_copy(
            src_ref=own_ref.at[fields, pl.ds(first, size), target],
            dst_ref=all_ref.at[fields, pl.ds(first, size), me],
            send_sem=part_send.at[number, step - 1],
            recv_sem=part_recv.at[number, step - 1],
            device_id=(target, brick),
            device_id_type=MESH,
        )

    def is_first(step):
        return (lax.rem(me + step, n_sec) == 0).astype(jnp.int32)

    def filtered(fields, values):
        inner = []
        for value in values:
            upper, lower = split(value.reshape(snaps * rows, cells))
            inner.append(fast(jnp.concatenate([upper, lower, upper], axis=1), cross_ref[...]))
        half = groups * batch
        results = []
        for value in inner:
            upper, lower = split(value)
            blocks = []
            for start in range(0, snaps * rows, width):
                high_part, low_part = upper[start : start + width], lower[start : start + width]
                outer = fast(rows_ref[...], jnp.concatenate([high_part, low_part, high_part], axis=0))
                joined = jnp.concatenate([outer[:half], outer[half:]], axis=1)
                blocks.append(joined.reshape(groups, batch, 2 * reduced))
            results.append(jnp.concatenate(blocks, axis=1))
        if fields[0] == 0:
            pl.semaphore_wait(barrier, len(near) + n_sec - 1)
        for field, joined in zip(fields, results):
            halo_out[0, field] = joined[0].astype(BF16)
            halo_out[1, field] = joined[groups - 1].astype(BF16)
            edge_ref[field, 0] = joined[1]
            edge_ref[field, 1] = joined[groups - 2]
            for group in range(1, groups - 3):
                own_ref[field, group // n_sec, group % n_sec] = joined[group + 1].astype(BF16)
        number = fields[0] // GROUP
        halo_copy(number, 0).start()
        halo_copy(number, 1).start()
        if held > 1:
            for step in range(1, n_sec):
                part_copy(number, step, is_first(step), held - 1).start()

    def finish(number):
        fields = range(number * GROUP, (number + 1) * GROUP)
        halo_copy(number, 1).wait_recv()
        halo_copy(number, 0).wait_recv()
        for field in fields:
            own_ref[field, 0, 0] = (edge_ref[field, 0] + halo_in[0, field].astype(F32)).astype(BF16)
            own_ref[field, held - 1, n_sec - 1] = (
                edge_ref[field, 1] + halo_in[1, field].astype(F32)
            ).astype(BF16)
        for step in range(1, n_sec):
            part_copy(number, step, (held - 1) * (1 - is_first(step)), 1).start()
        for field in fields:
            for piece in range(held):
                all_ref[field, piece, me] = own_ref[field, piece, me]

    for copy in loads:
        copy.wait()

    def source(field):
        if field < 3:
            return field_ref[field]
        number = field - 3
        one = number // 3 + number // 5
        two = number - 3 * one + one * (one - 1) // 2 + one
        return field_ref[one] * field_ref[two]

    for number in range(FIELDS // GROUP):
        fields = list(range(number * GROUP, (number + 1) * GROUP))
        filtered(fields, [source(field) for field in fields])
        if number > 0:
            finish(number - 1)
    finish(FIELDS // GROUP - 1)

    count = n_sec * snaps
    gram = jnp.zeros((count, count), F32)
    for field in range(FIELDS):
        if field % GROUP == 0:
            for step in range(1, n_sec):
                part_copy(field // GROUP, step, 0, held).wait_recv()
        for piece in range(held):
            block = all_ref[field, piece].reshape(count, 2 * reduced)
            gram = gram + fast(block, block, ((1,), (1,)))

    half = count // 4
    gram_out[0] = jnp.concatenate([gram[:half], gram[half : 2 * half]], axis=1)
    gram_out[1] = jnp.concatenate([gram[2 * half : 3 * half], gram[3 * half :]], axis=1)
    copies = []

    def send(source, landing, sender, receiver, device):
        copy = pltpu.make_async_remote_copy(
            src_ref=source, dst_ref=landing, send_sem=sender, recv_sem=receiver,
            device_id=device, device_id_type=MESH,
        )
        copy.start()
        copies.append(copy)
        return copy

    send(
        gram_out.at[1 - core], core_in, core_send.at[0], core_recv.at[0], (me, partner)
    ).wait_recv()
    total = gram_out[core] + core_in[...]
    offset = 0
    for digit, peers in stages:
        z_in[offset + digit] = total
        landed = [
            send(
                z_in.at[offset + digit], z_in.at[offset + digit],
                z_send.at[offset + step], z_recv.at[offset + step], (me, peer),
            )
            for step, peer in enumerate(peers)
        ]
        for copy in landed:
            copy.wait_recv()
        total = z_in[offset]
        for slot in range(1, len(peers) + 1):
            total = total + z_in[offset + slot]
        offset += len(peers) + 1
    sec_in[me] = total
    landed = [
        send(
            sec_in.at[me], sec_in.at[me], sec_send.at[step - 1], sec_recv.at[step - 1],
            (lax.rem(me + step, n_sec), brick),
        )
        for step in range(1, n_sec)
    ]
    for copy in landed:
        copy.wait_recv()
    total = sec_in[0]
    for slot in range(1, n_sec):
        total = total + sec_in[slot]
    total_ref[core] = total
    send(
        total_ref.at[core], total_ref.at[core], core_send.at[1], core_recv.at[1], (me, partner)
    ).wait_recv()
    first, second = total_ref[0], total_ref[1]
    gram = jnp.concatenate(
        [first[:, :count], first[:, count:], second[:, :count], second[:, count:]], axis=0
    )

    half = count // 2
    lower_bases, _ = merge_bases([gram[:half, :half], gram[half:, half:]], start_ref[0].T)
    blank = jnp.zeros_like(lower_bases[0])
    blocks = jnp.concatenate(
        [
            jnp.concatenate([lower_bases[0], blank], axis=1),
            jnp.concatenate([blank, lower_bases[1]], axis=1),
        ],
        axis=0,
    )
    top = exact(blocks, exact(gram, blocks), ((0,), (0,)))
    (coeffs,), (covariance,) = merge_bases([top], start_ref[1].T)
    weights = exact(coeffs, blocks, ((0,), (1,)))
    upper, lower = split(weights)
    weights = jnp.concatenate([upper, lower], axis=0)
    shape = (share, snaps)
    pick = (
        lax.broadcasted_iota(jnp.int32, shape, 1)
        == lax.broadcasted_iota(jnp.int32, shape, 0) + me * share
    ).astype(F32)
    energy_ref[...] = exact(pick, covariance) / total_values

    outs = []
    for piece in range(held):
        for field in range(FIELDS):
            block = all_ref[field, piece].reshape(count, 2 * reduced)
            values = fast(weights, block)
            piece_ref[:, field, :] = values[:snaps] + values[snaps:]
        sent_ref[piece] = piece_ref[...].astype(BF16)
        for step in range(1, n_sec):
            target = lax.rem(me + step, n_sec)
            copy = pltpu.make_async_remote_copy(
                src_ref=sent_ref.at[piece, pl.ds(target * share, share)],
                dst_ref=land_ref.at[piece, step - 1],
                send_sem=out_send.at[piece, step - 1],
                recv_sem=out_recv.at[piece, step - 1],
                device_id=(target, brick),
                device_id_type=MESH,
            )
            copy.start()
            outs.append((piece, step, copy))
        place = pl.ds(pl.multiple_of((piece * n_sec + me) * 2 * reduced, 2 * reduced), 2 * reduced)
        out_ref[:, :, place] = piece_ref[pl.ds(me * share, share)]

    for number in range(FIELDS // GROUP):
        for side in range(2):
            halo_copy(number, side).wait_send()
        for step in range(1, n_sec):
            part_copy(number, step, 0, held).wait_send()

    for copy in copies:
        copy.wait_send()
    for piece, step, copy in outs:
        copy.wait_recv()
        source = lax.rem(me + n_sec - step, n_sec)
        place = pl.ds(
            pl.multiple_of((piece * n_sec + source) * 2 * reduced, 2 * reduced), 2 * reduced
        )
        out_ref[:, :, place] = land_ref[piece, step - 1].astype(F32)
    for _, _, copy in outs:
        copy.wait_send()


def per_device(n_sec, n_brick, velocity, filter_taps, start_vectors):
    _, snaps, rows, cells = velocity.shape
    reduced = cells // 4
    groups = rows // 4 + 2
    share = snaps // n_sec
    held = rows // 4 // n_sec
    slots = max(sum(radix for _, radix in radices(n_brick // 2)), 1)
    sets = FIELDS // GROUP
    count = n_sec * snaps
    batch = max(1, min(snaps, 256 // rows))
    total_values = n_sec * snaps * FIELDS * (rows // 2) * reduced * n_brick
    width = 2 * reduced
    dma = pltpu.SemaphoreType.DMA
    return pl.pallas_call(
        functools.partial(kernel, n_sec, n_brick, total_values),
        out_shape=(
            jax.ShapeDtypeStruct((share, FIELDS, rows // 2 * reduced), F32),
            jax.ShapeDtypeStruct((share, snaps), F32),
        ),
        in_specs=[
            pl.BlockSpec(memory_space=pl.ANY),
            pl.BlockSpec(memory_space=pltpu.SMEM),
            pl.BlockSpec(memory_space=pltpu.VMEM),
        ],
        out_specs=(
            pl.BlockSpec(memory_space=pltpu.VMEM),
            pl.BlockSpec(memory_space=pltpu.VMEM),
        ),
        scratch_shapes=[
            pltpu.VMEM((3, snaps, rows, cells), F32),
            pltpu.VMEM((3 * cells, reduced), BF16),
            pltpu.VMEM((2 * groups * batch, 3 * batch * rows), BF16),
            pltpu.VMEM((FIELDS, 2, snaps, width), F32),
            pltpu.VMEM((2, FIELDS, snaps, width), BF16),
            pltpu.VMEM((2, FIELDS, snaps, width), BF16),
            pltpu.VMEM((FIELDS, held, n_sec, snaps, width), BF16),
            pltpu.VMEM((FIELDS, held, n_sec, snaps, width), BF16),
            pltpu.VMEM((2, count // 4, 2 * count), F32),
            pltpu.VMEM((count // 4, 2 * count), F32),
            pltpu.VMEM((slots, count // 4, 2 * count), F32),
            pltpu.VMEM((n_sec, count // 4, 2 * count), F32),
            pltpu.VMEM((2, count // 4, 2 * count), F32),
            pltpu.VMEM((snaps, FIELDS, width), F32),
            pltpu.VMEM((held, snaps, FIELDS, width), BF16),
            pltpu.VMEM((held, n_sec - 1, share, FIELDS, width), BF16),
            dma((3,)),
            dma((sets, 2)),
            dma((sets, 2)),
            dma((sets, n_sec - 1)),
            dma((sets, n_sec - 1)),
            dma((2,)),
            dma((2,)),
            dma((slots,)),
            dma((slots,)),
            dma((n_sec - 1,)),
            dma((n_sec - 1,)),
            dma((held, n_sec - 1)),
            dma((held, n_sec - 1)),
        ],
        compiler_params=pltpu.CompilerParams(
            collective_id=0, has_side_effects=True, vmem_limit_bytes=60 * 1024 * 1024
        ),
    )(velocity, filter_taps, jnp.transpose(start_vectors, (0, 2, 1)))


def solution(mesh):
    in_specs = (P(None, "sec", "brick", None), P(), P())
    out_specs = (P("sec", None, "brick"), P("sec", None))
    return jax.shard_map(
        functools.partial(per_device, mesh.shape["sec"], mesh.shape["brick"]),
        mesh=mesh, in_specs=in_specs, out_specs=out_specs, check_vma=False,
    )
```

```python
import functools

import jax
import jax.numpy as jnp
from jax import lax
from jax.experimental import pallas as pl
from jax.experimental.pallas import tpu as pltpu
from jax.sharding import PartitionSpec as P

CY = 32
CZ = 24
NS_STEPS = 8
TAPS = 9
FIELDS = 9
GROUP = 3
LANES = 128
MESH = pl.DeviceIdType.MESH
F32 = jnp.float32
BF16 = jnp.bfloat16


def exact(a, b, dims=((1,), (0,))):
    return lax.dot_general(
        a, b, (dims, ((), ())), precision=lax.Precision.HIGHEST, preferred_element_type=F32
    )


def fast(a, b, dims=((1,), (0,))):
    return lax.dot_general(a, b, (dims, ((), ())), preferred_element_type=F32)


def split(value):
    high = value.astype(BF16)
    return high, (value - high.astype(F32)).astype(BF16)


def grid_of(shape, dim):
    return lax.broadcasted_iota(jnp.int32, shape, dim).astype(F32)


def eye_of(size):
    shape = (size, size)
    return (
        lax.broadcasted_iota(jnp.int32, shape, 0) == lax.broadcasted_iota(jnp.int32, shape, 1)
    ).astype(F32)


def trace_of(matrix):
    return jnp.sum(matrix * eye_of(matrix.shape[0]), keepdims=True)


def pick_taps(taps_ref, dim, offset):
    total = jnp.zeros_like(offset)
    for tap in range(TAPS):
        total = jnp.where(offset == float(tap), taps_ref[dim, tap], total)
    return total


def radices(size):
    result, stride = [], 1
    while size > 1:
        radix = 4 if size % 4 == 0 else 2
        result.append((stride, radix))
        stride, size = stride * radix, size // radix
    return result


def terms(value):
    first = value.astype(BF16)
    rest = value - first.astype(F32)
    second = rest.astype(BF16)
    last = rest - second.astype(F32)
    return first, second, last.astype(BF16), rest, last


def as_left(value, order):
    slot = lax.broadcasted_iota(jnp.int32, value.shape, 1) // order
    _, _, _, rest, last = terms(value)
    return jnp.where(slot < 3, value, jnp.where(slot < 5, rest, last)).astype(BF16)


def as_right(value):
    first, second, third, _, _ = terms(value)
    blocks = [first, second, third, first, second, first]
    blank = jnp.zeros_like(first)
    spare = LANES // value.shape[0] - len(blocks)
    return jnp.concatenate(blocks + [blank] * spare, axis=0)


def narrow(left, right):
    return fast(as_left(left, right.shape[0]), as_right(right))


def newton_factors(matrices, scales):
    order = matrices[0].shape[0]
    shape = (order, LANES)
    unit = (
        lax.broadcasted_iota(jnp.int32, shape, 0)
        == lax.rem(lax.broadcasted_iota(jnp.int32, shape, 1), order)
    ).astype(F32)
    gaps = [unit - m / s for m, s in zip(matrices, scales)]
    factors = [unit + 0.5 * v for v in gaps]
    products = factors
    for step in range(NS_STEPS - 1):
        squares = [narrow(v, v) for v in gaps]
        gaps = [narrow(w, 0.75 * unit + 0.25 * v) for w, v in zip(squares, gaps)]
        factors = [unit + 0.5 * v for v in gaps]
        if step < NS_STEPS - 2:
            products = [narrow(z, e) for z, e in zip(products, factors)]
    return [(z, e, 1.0 / jnp.sqrt(s)) for z, e, s in zip(products, factors, scales)]


def times_root(value, root):
    product, factor, scale = root
    return narrow(narrow(value, product) * scale, factor)


def root_times(value, root):
    product, factor, scale = root
    return narrow(factor, narrow(product, value) * scale)


def total_of(value, copies):
    total = jnp.sum(jnp.sum(value, axis=0, keepdims=True), axis=1, keepdims=True)
    return total * (1.0 / copies)


def merge_bases(grams, wides, start, start_t):
    size = grams[0].shape[0]
    copies = LANES // start_t.shape[0]
    traces = [trace_of(g) for g in grams]
    shares = [1.0 / t for t in traces]
    basis = [exact(g, start) * s for g, s in zip(grams, shares)]
    basis_t = [exact(start_t, w) * s for w, s in zip(wides, shares)]
    for repeat in range(2):
        metric = [exact(t[:, :size], b) for t, b in zip(basis_t, basis)]
        scales = [total_of(b * b, copies) for b in basis]
        image = [exact(g, b) * s for g, b, s in zip(grams, basis, shares)]
        image_t = [exact(t[:, :size], w) * s for t, w, s in zip(basis_t, wides, shares)]
        roots = newton_factors(metric, scales)
        if repeat == 0:
            basis = [times_root(b, r) for b, r in zip(image, roots)]
            basis_t = [root_times(t, r) for t, r in zip(image_t, roots)]
    basis = [times_root(b, r) for b, r in zip(basis, roots)]
    basis_t = [root_times(t, r) for t, r in zip(basis_t, roots)]
    image = [times_root(b, r) for b, r in zip(image, roots)]
    image_t = [root_times(t, r) for t, r in zip(image_t, roots)]
    metric = [exact(t[:, :size], b) for t, b in zip(basis_t, image)]
    scales = [total_of(q * b, copies) for q, b in zip(basis, image)]
    roots = newton_factors(metric, scales)
    project = [times_root(q, r) for q, r in zip(basis, roots)]
    project_t = [root_times(t, r) for t, r in zip(basis_t, roots)]
    image = [times_root(b, r) for b, r in zip(image, roots)]
    image_t = [root_times(t, r) for t, r in zip(image_t, roots)]
    metric = [exact(t[:, :size], b) for t, b in zip(image_t, image)]
    scales = [total_of(b * b, copies) for b in image]
    spread = [narrow(p, m) for p, m in zip(project, metric)]
    spread_t = [narrow(m, t) for t, m in zip(project_t, metric)]
    roots = newton_factors(metric, scales)
    coeffs = [times_root(p, r) for p, r in zip(spread, roots)]
    coeffs_t = [root_times(t, r) for t, r in zip(spread_t, roots)]
    covariance = [m * t for m, t in zip(metric, traces)]
    return coeffs, coeffs_t, covariance


def merge_tree(gram, starts, starts_t):
    order, size = starts_t[0].shape
    columns = [gram[:, part : part + size] for part in range(0, gram.shape[0], size)]
    grams = [column[part * size : (part + 1) * size] for part, column in enumerate(columns)]
    wides = [jnp.concatenate([g] * (LANES // size), axis=1) for g in grams]
    lower, lower_t, _ = merge_bases(grams, wides, starts[0], starts_t[0])
    images = [exact(column, basis) for column, basis in zip(columns, lower)]
    lane = lax.broadcasted_iota(jnp.int32, (order, LANES), 1)
    own = lax.rem(lane, size) < order
    rows = []
    for part, basis_t in enumerate(lower_t):
        left, right = [
            exact(basis_t[:, :size], image[part * size : (part + 1) * size]) for image in images
        ]
        rows.append(jnp.where(own, left, right))
    wide = jnp.concatenate(rows, axis=0)
    (_,), (coeffs_t,), (covariance,) = merge_bases([wide[:, :size]], [wide], starts[1], starts_t[1])
    joined = jnp.concatenate(
        [
            jnp.where((lane >= part * size) & (lane < (part + 1) * size), basis_t, 0.0)
            for part, basis_t in enumerate(lower_t)
        ],
        axis=0,
    )
    weights = exact(coeffs_t[:, :size], joined)
    return weights[:, : 2 * size], covariance[:, :order]


def kernel(
    n_sec, n_brick, total_values,
    velocity_ref, taps_ref, start_ref,
    out_ref, energy_ref,
    field_ref, cross_ref, rows_ref, edge_ref, halo_out, halo_in, own_ref, all_ref,
    wide_ref, gram_out, core_in, z_in, sec_in, total_ref, piece_ref, sent_ref, land_ref,
    load_sem, halo_send, halo_recv, part_send, part_recv,
    core_send, core_recv, z_send, z_recv, sec_send, sec_recv, out_send, out_recv,
):
    snaps, rows = velocity_ref.shape[1], velocity_ref.shape[2]
    cells = velocity_ref.shape[3]
    reduced = cells // 4
    groups = rows // 4 + 2
    batch = rows_ref.shape[0] // (2 * groups)
    share = snaps // n_sec
    held = own_ref.shape[1]
    me = lax.axis_index("sec")
    brick = lax.axis_index("brick")
    low = lax.rem(brick + n_brick - 1, n_brick)
    high = lax.rem(brick + 1, n_brick)
    core = lax.rem(brick, 2)
    partner = brick + 1 - 2 * core
    stages = []
    for stride, radix in radices(n_brick // 2):
        digit = lax.rem(brick // (2 * stride), radix)
        peers = [
            brick + 2 * stride * (lax.rem(digit + step, radix) - digit) for step in range(1, radix)
        ]
        stages.append((digit, peers))
    near = [low, high] + [peer for _, peers in stages for peer in peers]

    loads = []
    for number in range(3):
        copy = pltpu.make_async_copy(
            velocity_ref.at[number], field_ref.at[number], load_sem.at[number]
        )
        copy.start()
        loads.append(copy)

    barrier = pltpu.get_barrier_semaphore()
    for target in near:
        pl.semaphore_signal(barrier, inc=1, device_id=(me, target), device_id_type=MESH)
    for step in range(1, n_sec):
        pl.semaphore_signal(
            barrier, inc=1, device_id=(lax.rem(me + step, n_sec), brick), device_id_type=MESH
        )

    for level in range(2):
        wide_ref[level] = jnp.concatenate([start_ref[level].T] * (LANES // snaps), axis=1)

    shape = (cells, reduced)
    cell, point = grid_of(shape, 0), grid_of(shape, 1)
    y = jnp.floor((cell + 0.5) * (1.0 / CZ))
    z = cell - y * CZ
    j = jnp.floor((point + 0.5) * (2.0 / CZ))
    k = point - j * (CZ // 2)
    off_y = y - 2.0 * j + 4.0
    off_y = jnp.where(off_y < 0.0, off_y + CY, off_y)
    off_y = jnp.where(off_y >= CY, off_y - CY, off_y)
    off_z = z - 2.0 * k + 4.0
    off_z = jnp.where(off_z < 0.0, off_z + CZ, off_z)
    off_z = jnp.where(off_z >= CZ, off_z - CZ, off_z)
    upper, lower = split(pick_taps(taps_ref, 1, off_y) * pick_taps(taps_ref, 2, off_z))
    cross_ref[0:cells, :] = upper
    cross_ref[cells : 2 * cells, :] = upper
    cross_ref[2 * cells :, :] = lower

    shape = (2 * groups * batch, batch * rows)
    target, source = grid_of(shape, 0), grid_of(shape, 1)
    parity = (target >= groups * batch).astype(F32)
    rest = target - parity * (groups * batch)
    pair = jnp.floor((rest + 0.5) * (1.0 / batch))
    snap = rest - pair * batch
    snap_in = jnp.floor((source + 0.5) * (1.0 / rows))
    offset = (source - snap_in * rows) - 2.0 * (2.0 * pair + parity - 2.0) + 4.0
    offset = jnp.where(snap == snap_in, offset, -1.0)
    upper, lower = split(pick_taps(taps_ref, 0, offset))
    width = batch * rows
    rows_ref[:, 0:width] = upper
    rows_ref[:, width : 2 * width] = upper
    rows_ref[:, 2 * width :] = lower

    def halo_copy(number, side):
        fields = pl.ds(number * GROUP, GROUP)
        return pltpu.make_async_remote_copy(
            src_ref=halo_out.at[side, fields],
            dst_ref=halo_in.at[1 - side, fields],
            send_sem=halo_send.at[number, side],
            recv_sem=halo_recv.at[number, 1 - side],
            device_id=(me, low if side == 0 else high),
            device_id_type=MESH,
        )

    def part_copy(number, step, first, size):
        fields = pl.ds(number * GROUP, GROUP)
        target = lax.rem(me + step, n_sec)
        return pltpu.make_async_remote_copy(
            src_ref=own_ref.at[fields, pl.ds(first, size), target],
            dst_ref=all_ref.at[fields, pl.ds(first, size), me],
            send_sem=part_send.at[number, step - 1],
            recv_sem=part_recv.at[number, step - 1],
            device_id=(target, brick),
            device_id_type=MESH,
        )

    def is_first(step):
        return (lax.rem(me + step, n_sec) == 0).astype(jnp.int32)

    def filtered(fields, values):
        inner = []
        for value in values:
            upper, lower = split(value.reshape(snaps * rows, cells))
            inner.append(fast(jnp.concatenate([upper, lower, upper], axis=1), cross_ref[...]))
        half = groups * batch
        results = []
        for value in inner:
            upper, lower = split(value)
            blocks = []
            for start in range(0, snaps * rows, width):
                high_part, low_part = upper[start : start + width], lower[start : start + width]
                outer = fast(rows_ref[...], jnp.concatenate([high_part, low_part, high_part], axis=0))
                joined = jnp.concatenate([outer[:half], outer[half:]], axis=1)
                blocks.append(joined.reshape(groups, batch, 2 * reduced))
            results.append(jnp.concatenate(blocks, axis=1))
        if fields[0] == 0:
            pl.semaphore_wait(barrier, len(near) + n_sec - 1)
        for field, joined in zip(fields, results):
            halo_out[0, field] = joined[0].astype(BF16)
            halo_out[1, field] = joined[groups - 1].astype(BF16)
            edge_ref[field, 0] = joined[1]
            edge_ref[field, 1] = joined[groups - 2]
            for group in range(1, groups - 3):
                own_ref[field, group // n_sec, group % n_sec] = joined[group + 1].astype(BF16)
        number = fields[0] // GROUP
        halo_copy(number, 0).start()
        halo_copy(number, 1).start()
        if held > 1:
            for step in range(1, n_sec):
                part_copy(number, step, is_first(step), held - 1).start()

    def finish(number):
        fields = range(number * GROUP, (number + 1) * GROUP)
        halo_copy(number, 1).wait_recv()
        halo_copy(number, 0).wait_recv()
        for field in fields:
            own_ref[field, 0, 0] = (edge_ref[field, 0] + halo_in[0, field].astype(F32)).astype(BF16)
            own_ref[field, held - 1, n_sec - 1] = (
                edge_ref[field, 1] + halo_in[1, field].astype(F32)
            ).astype(BF16)
        for step in range(1, n_sec):
            part_copy(number, step, (held - 1) * (1 - is_first(step)), 1).start()
        for field in fields:
            for piece in range(held):
                all_ref[field, piece, me] = own_ref[field, piece, me]

    for copy in loads:
        copy.wait()

    def source(field):
        if field < 3:
            return field_ref[field]
        number = field - 3
        one = number // 3 + number // 5
        two = number - 3 * one + one * (one - 1) // 2 + one
        return field_ref[one] * field_ref[two]

    for number in range(FIELDS // GROUP):
        fields = list(range(number * GROUP, (number + 1) * GROUP))
        filtered(fields, [source(field) for field in fields])
        if number > 0:
            finish(number - 1)
    finish(FIELDS // GROUP - 1)

    count = n_sec * snaps
    gram = jnp.zeros((count, count), F32)
    for field in range(FIELDS):
        if field % GROUP == 0:
            for step in range(1, n_sec):
                part_copy(field // GROUP, step, 0, held).wait_recv()
        for piece in range(held):
            block = all_ref[field, piece].reshape(count, 2 * reduced)
            gram = gram + fast(block, block, ((1,), (1,)))

    half = count // 4
    gram_out[0] = jnp.concatenate([gram[:half], gram[half : 2 * half]], axis=1)
    gram_out[1] = jnp.concatenate([gram[2 * half : 3 * half], gram[3 * half :]], axis=1)
    copies = []

    def send(source, landing, sender, receiver, device):
        copy = pltpu.make_async_remote_copy(
            src_ref=source, dst_ref=landing, send_sem=sender, recv_sem=receiver,
            device_id=device, device_id_type=MESH,
        )
        copy.start()
        copies.append(copy)
        return copy

    send(
        gram_out.at[1 - core], core_in, core_send.at[0], core_recv.at[0], (me, partner)
    ).wait_recv()
    total = gram_out[core] + core_in[...]
    offset = 0
    for digit, peers in stages:
        z_in[offset + digit] = total
        landed = [
            send(
                z_in.at[offset + digit], z_in.at[offset + digit],
                z_send.at[offset + step], z_recv.at[offset + step], (me, peer),
            )
            for step, peer in enumerate(peers)
        ]
        for copy in landed:
            copy.wait_recv()
        total = z_in[offset]
        for slot in range(1, len(peers) + 1):
            total = total + z_in[offset + slot]
        offset += len(peers) + 1
    sec_in[me] = total
    landed = [
        send(
            sec_in.at[me], sec_in.at[me], sec_send.at[step - 1], sec_recv.at[step - 1],
            (lax.rem(me + step, n_sec), brick),
        )
        for step in range(1, n_sec)
    ]
    for copy in landed:
        copy.wait_recv()
    total = sec_in[0]
    for slot in range(1, n_sec):
        total = total + sec_in[slot]
    total_ref[core] = total
    send(
        total_ref.at[core], total_ref.at[core], core_send.at[1], core_recv.at[1], (me, partner)
    ).wait_recv()
    first, second = total_ref[0], total_ref[1]
    gram = jnp.concatenate(
        [first[:, :count], first[:, count:], second[:, :count], second[:, count:]], axis=0
    )

    weights, covariance = merge_tree(
        gram, [wide_ref[0], wide_ref[1]], [start_ref[0], start_ref[1]]
    )
    upper, lower = split(weights)
    weights = jnp.concatenate([upper, lower], axis=0)
    shape = (share, snaps)
    pick = (
        lax.broadcasted_iota(jnp.int32, shape, 1)
        == lax.broadcasted_iota(jnp.int32, shape, 0) + me * share
    ).astype(F32)
    energy_ref[...] = exact(pick, covariance) / total_values

    outs = []
    for piece in range(held):
        for field in range(FIELDS):
            block = all_ref[field, piece].reshape(count, 2 * reduced)
            values = fast(weights, block)
            piece_ref[:, field, :] = values[:snaps] + values[snaps:]
        sent_ref[piece] = piece_ref[...].astype(BF16)
        for step in range(1, n_sec):
            target = lax.rem(me + step, n_sec)
            copy = pltpu.make_async_remote_copy(
                src_ref=sent_ref.at[piece, pl.ds(target * share, share)],
                dst_ref=land_ref.at[piece, step - 1],
                send_sem=out_send.at[piece, step - 1],
                recv_sem=out_recv.at[piece, step - 1],
                device_id=(target, brick),
                device_id_type=MESH,
            )
            copy.start()
            outs.append((piece, step, copy))
        place = pl.ds(pl.multiple_of((piece * n_sec + me) * 2 * reduced, 2 * reduced), 2 * reduced)
        out_ref[:, :, place] = piece_ref[pl.ds(me * share, share)]

    for number in range(FIELDS // GROUP):
        for side in range(2):
            halo_copy(number, side).wait_send()
        for step in range(1, n_sec):
            part_copy(number, step, 0, held).wait_send()

    for copy in copies:
        copy.wait_send()
    for piece, step, copy in outs:
        copy.wait_recv()
        source = lax.rem(me + n_sec - step, n_sec)
        place = pl.ds(
            pl.multiple_of((piece * n_sec + source) * 2 * reduced, 2 * reduced), 2 * reduced
        )
        out_ref[:, :, place] = land_ref[piece, step - 1].astype(F32)
    for _, _, copy in outs:
        copy.wait_send()


def per_device(n_sec, n_brick, velocity, filter_taps, start_vectors):
    _, snaps, rows, cells = velocity.shape
    reduced = cells // 4
    groups = rows // 4 + 2
    share = snaps // n_sec
    held = rows // 4 // n_sec
    slots = max(sum(radix for _, radix in radices(n_brick // 2)), 1)
    sets = FIELDS // GROUP
    count = n_sec * snaps
    batch = max(1, min(snaps, 256 // rows))
    total_values = n_sec * snaps * FIELDS * (rows // 2) * reduced * n_brick
    width = 2 * reduced
    dma = pltpu.SemaphoreType.DMA
    return pl.pallas_call(
        functools.partial(kernel, n_sec, n_brick, total_values),
        out_shape=(
            jax.ShapeDtypeStruct((share, FIELDS, rows // 2 * reduced), F32),
            jax.ShapeDtypeStruct((share, snaps), F32),
        ),
        in_specs=[
            pl.BlockSpec(memory_space=pl.ANY),
            pl.BlockSpec(memory_space=pltpu.SMEM),
            pl.BlockSpec(memory_space=pltpu.VMEM),
        ],
        out_specs=(
            pl.BlockSpec(memory_space=pltpu.VMEM),
            pl.BlockSpec(memory_space=pltpu.VMEM),
        ),
        scratch_shapes=[
            pltpu.VMEM((3, snaps, rows, cells), F32),
            pltpu.VMEM((3 * cells, reduced), BF16),
            pltpu.VMEM((2 * groups * batch, 3 * batch * rows), BF16),
            pltpu.VMEM((FIELDS, 2, snaps, width), F32),
            pltpu.VMEM((2, FIELDS, snaps, width), BF16),
            pltpu.VMEM((2, FIELDS, snaps, width), BF16),
            pltpu.VMEM((FIELDS, held, n_sec, snaps, width), BF16),
            pltpu.VMEM((FIELDS, held, n_sec, snaps, width), BF16),
            pltpu.VMEM((2, 2 * snaps, LANES), F32),
            pltpu.VMEM((2, count // 4, 2 * count), F32),
            pltpu.VMEM((count // 4, 2 * count), F32),
            pltpu.VMEM((slots, count // 4, 2 * count), F32),
            pltpu.VMEM((n_sec, count // 4, 2 * count), F32),
            pltpu.VMEM((2, count // 4, 2 * count), F32),
            pltpu.VMEM((snaps, FIELDS, width), F32),
            pltpu.VMEM((held, snaps, FIELDS, width), BF16),
            pltpu.VMEM((held, n_sec - 1, share, FIELDS, width), BF16),
            dma((3,)),
            dma((sets, 2)),
            dma((sets, 2)),
            dma((sets, n_sec - 1)),
            dma((sets, n_sec - 1)),
            dma((2,)),
            dma((2,)),
            dma((slots,)),
            dma((slots,)),
            dma((n_sec - 1,)),
            dma((n_sec - 1,)),
            dma((held, n_sec - 1)),
            dma((held, n_sec - 1)),
        ],
        compiler_params=pltpu.CompilerParams(
            collective_id=0, has_side_effects=True, vmem_limit_bytes=60 * 1024 * 1024
        ),
    )(velocity, filter_taps, jnp.transpose(start_vectors, (0, 2, 1)))


def solution(mesh):
    in_specs = (P(None, "sec", "brick", None), P(), P())
    out_specs = (P("sec", None, "brick"), P("sec", None))
    return jax.shard_map(
        functools.partial(per_device, mesh.shape["sec"], mesh.shape["brick"]),
        mesh=mesh, in_specs=in_specs, out_specs=out_specs, check_vma=False,
    )
```

```python
import functools

import jax
import jax.numpy as jnp
from jax import lax
from jax.experimental import pallas as pl
from jax.experimental.pallas import tpu as pltpu
from jax.sharding import PartitionSpec as P

CY = 32
CZ = 24
NS_STEPS = 8
TAPS = 9
FIELDS = 9
GROUP = 3
LANES = 128
MESH = pl.DeviceIdType.MESH
F32 = jnp.float32
BF16 = jnp.bfloat16


def exact(a, b, dims=((1,), (0,))):
    return lax.dot_general(
        a, b, (dims, ((), ())), precision=lax.Precision.HIGHEST, preferred_element_type=F32
    )


def fast(a, b, dims=((1,), (0,))):
    return lax.dot_general(a, b, (dims, ((), ())), preferred_element_type=F32)


def split(value):
    high = value.astype(BF16)
    return high, (value - high.astype(F32)).astype(BF16)


def grid_of(shape, dim):
    return lax.broadcasted_iota(jnp.int32, shape, dim).astype(F32)


def eye_of(size):
    shape = (size, size)
    return (
        lax.broadcasted_iota(jnp.int32, shape, 0) == lax.broadcasted_iota(jnp.int32, shape, 1)
    ).astype(F32)


def trace_of(matrix):
    return jnp.sum(matrix * eye_of(matrix.shape[0]), keepdims=True)


def pick_taps(taps_ref, dim, offset):
    total = jnp.zeros_like(offset)
    for tap in range(TAPS):
        total = jnp.where(offset == float(tap), taps_ref[dim, tap], total)
    return total


def radices(size):
    result, stride = [], 1
    while size > 1:
        radix = 4 if size % 4 == 0 else 2
        result.append((stride, radix))
        stride, size = stride * radix, size // radix
    return result


def terms(value):
    first = value.astype(BF16)
    rest = value - first.astype(F32)
    second = rest.astype(BF16)
    last = rest - second.astype(F32)
    return first, second, last.astype(BF16), rest, last


def as_left(value, order):
    slot = lax.broadcasted_iota(jnp.int32, value.shape, 1) // order
    _, _, _, rest, last = terms(value)
    return jnp.where(slot < 3, value, jnp.where(slot < 5, rest, last)).astype(BF16)


def as_right(value):
    first, second, third, _, _ = terms(value)
    blocks = [first, second, third, first, second, first]
    blank = jnp.zeros_like(first)
    spare = LANES // value.shape[0] - len(blocks)
    return jnp.concatenate(blocks + [blank] * spare, axis=0)


def narrow(left, right):
    return fast(as_left(left, right.shape[0]), as_right(right))


def newton_factors(matrices, scales):
    order = matrices[0].shape[0]
    shape = (order, LANES)
    unit = (
        lax.broadcasted_iota(jnp.int32, shape, 0)
        == lax.rem(lax.broadcasted_iota(jnp.int32, shape, 1), order)
    ).astype(F32)
    gaps = [unit - m / s for m, s in zip(matrices, scales)]
    factors = [unit + 0.5 * v for v in gaps]
    products = factors
    for step in range(NS_STEPS - 1):
        squares = [narrow(v, v) for v in gaps]
        gaps = [narrow(w, 0.75 * unit + 0.25 * v) for w, v in zip(squares, gaps)]
        factors = [unit + 0.5 * v for v in gaps]
        if step < NS_STEPS - 2:
            products = [narrow(z, e) for z, e in zip(products, factors)]
    return [(z, e, 1.0 / jnp.sqrt(s)) for z, e, s in zip(products, factors, scales)]


def times_root(value, root):
    product, factor, scale = root
    return narrow(narrow(value, product) * scale, factor)


def root_times(value, root):
    product, factor, scale = root
    return narrow(factor, narrow(product, value) * scale)


def total_of(value, copies):
    total = jnp.sum(jnp.sum(value, axis=0, keepdims=True), axis=1, keepdims=True)
    return total * (1.0 / copies)


def merge_bases(grams, wides, start, start_t):
    size = grams[0].shape[0]
    copies = LANES // start_t.shape[0]
    traces = [trace_of(g) for g in grams]
    shares = [1.0 / t for t in traces]
    basis = [exact(g, start) * s for g, s in zip(grams, shares)]
    basis_t = [exact(start_t, w) * s for w, s in zip(wides, shares)]
    for repeat in range(2):
        metric = [exact(t[:, :size], b) for t, b in zip(basis_t, basis)]
        scales = [total_of(b * b, copies) for b in basis]
        image = [exact(g, b) * s for g, b, s in zip(grams, basis, shares)]
        image_t = [exact(t[:, :size], w) * s for t, w, s in zip(basis_t, wides, shares)]
        roots = newton_factors(metric, scales)
        if repeat == 0:
            basis = [times_root(b, r) for b, r in zip(image, roots)]
            basis_t = [root_times(t, r) for t, r in zip(image_t, roots)]
    basis = [times_root(b, r) for b, r in zip(basis, roots)]
    basis_t = [root_times(t, r) for t, r in zip(basis_t, roots)]
    image = [times_root(b, r) for b, r in zip(image, roots)]
    image_t = [root_times(t, r) for t, r in zip(image_t, roots)]
    metric = [exact(t[:, :size], b) for t, b in zip(basis_t, image)]
    scales = [total_of(q * b, copies) for q, b in zip(basis, image)]
    roots = newton_factors(metric, scales)
    project = [times_root(q, r) for q, r in zip(basis, roots)]
    project_t = [root_times(t, r) for t, r in zip(basis_t, roots)]
    image = [times_root(b, r) for b, r in zip(image, roots)]
    image_t = [root_times(t, r) for t, r in zip(image_t, roots)]
    metric = [exact(t[:, :size], b) for t, b in zip(image_t, image)]
    scales = [total_of(b * b, copies) for b in image]
    spread = [narrow(p, m) for p, m in zip(project, metric)]
    spread_t = [narrow(m, t) for t, m in zip(project_t, metric)]
    roots = newton_factors(metric, scales)
    coeffs = [times_root(p, r) for p, r in zip(spread, roots)]
    coeffs_t = [root_times(t, r) for t, r in zip(spread_t, roots)]
    covariance = [m * t for m, t in zip(metric, traces)]
    return coeffs, coeffs_t, covariance


def merge_tree(gram, starts, starts_t):
    order, size = starts_t[0].shape
    columns = [gram[:, part : part + size] for part in range(0, gram.shape[0], size)]
    grams = [column[part * size : (part + 1) * size] for part, column in enumerate(columns)]
    wides = [jnp.concatenate([g] * (LANES // size), axis=1) for g in grams]
    lower, lower_t, _ = merge_bases(grams, wides, starts[0], starts_t[0])
    images = [exact(column, basis) for column, basis in zip(columns, lower)]
    lane = lax.broadcasted_iota(jnp.int32, (order, LANES), 1)
    own = lax.rem(lane, size) < order
    rows = []
    for part, basis_t in enumerate(lower_t):
        left, right = [
            exact(basis_t[:, :size], image[part * size : (part + 1) * size]) for image in images
        ]
        rows.append(jnp.where(own, left, right))
    wide = jnp.concatenate(rows, axis=0)
    (_,), (coeffs_t,), (covariance,) = merge_bases([wide[:, :size]], [wide], starts[1], starts_t[1])
    joined = jnp.concatenate(
        [
            jnp.where(lax.rem(lane // size, len(lower_t)) == part, basis_t, 0.0)
            for part, basis_t in enumerate(lower_t)
        ],
        axis=0,
    )
    return exact(coeffs_t[:, :size], joined), covariance[:, :order]


def kernel(
    n_sec, n_brick, total_values,
    velocity_ref, taps_ref, start_ref,
    land_ref, energy_ref,
    field_ref, cross_ref, rows_ref, edge_ref, halo_out, halo_in, own_ref, all_ref,
    wide_ref, gram_out, core_in, z_in, sec_in, total_ref, sent_ref,
    load_sem, halo_send, halo_recv, part_send, part_recv,
    core_send, core_recv, z_send, z_recv, sec_send, sec_recv, out_send, out_recv,
):
    snaps, rows = velocity_ref.shape[1], velocity_ref.shape[2]
    cells = velocity_ref.shape[3]
    reduced = cells // 4
    groups = rows // 4 + 2
    batch = rows_ref.shape[0] // (2 * groups)
    share = snaps // n_sec
    held = own_ref.shape[1]
    me = lax.axis_index("sec")
    brick = lax.axis_index("brick")
    low = lax.rem(brick + n_brick - 1, n_brick)
    high = lax.rem(brick + 1, n_brick)
    core = lax.rem(brick, 2)
    partner = brick + 1 - 2 * core
    stages = []
    for stride, radix in radices(n_brick // 2):
        digit = lax.rem(brick // (2 * stride), radix)
        peers = [
            brick + 2 * stride * (lax.rem(digit + step, radix) - digit) for step in range(1, radix)
        ]
        stages.append((digit, peers))
    near = [low, high] + [peer for _, peers in stages for peer in peers]

    loads = []
    for number in range(3):
        copy = pltpu.make_async_copy(
            velocity_ref.at[number], field_ref.at[number], load_sem.at[number]
        )
        copy.start()
        loads.append(copy)

    barrier = pltpu.get_barrier_semaphore()
    for target in near:
        pl.semaphore_signal(barrier, inc=1, device_id=(me, target), device_id_type=MESH)
    for step in range(1, n_sec):
        pl.semaphore_signal(
            barrier, inc=1, device_id=(lax.rem(me + step, n_sec), brick), device_id_type=MESH
        )

    for level in range(2):
        wide_ref[level] = jnp.concatenate([start_ref[level].T] * (LANES // snaps), axis=1)

    shape = (cells, reduced)
    cell, point = grid_of(shape, 0), grid_of(shape, 1)
    y = jnp.floor((cell + 0.5) * (1.0 / CZ))
    z = cell - y * CZ
    j = jnp.floor((point + 0.5) * (2.0 / CZ))
    k = point - j * (CZ // 2)
    off_y = y - 2.0 * j + 4.0
    off_y = jnp.where(off_y < 0.0, off_y + CY, off_y)
    off_y = jnp.where(off_y >= CY, off_y - CY, off_y)
    off_z = z - 2.0 * k + 4.0
    off_z = jnp.where(off_z < 0.0, off_z + CZ, off_z)
    off_z = jnp.where(off_z >= CZ, off_z - CZ, off_z)
    upper, lower = split(pick_taps(taps_ref, 1, off_y) * pick_taps(taps_ref, 2, off_z))
    cross_ref[0:cells, :] = upper
    cross_ref[cells : 2 * cells, :] = upper
    cross_ref[2 * cells :, :] = lower

    shape = (2 * groups * batch, batch * rows)
    target, source = grid_of(shape, 0), grid_of(shape, 1)
    parity = (target >= groups * batch).astype(F32)
    rest = target - parity * (groups * batch)
    pair = jnp.floor((rest + 0.5) * (1.0 / batch))
    snap = rest - pair * batch
    snap_in = jnp.floor((source + 0.5) * (1.0 / rows))
    offset = (source - snap_in * rows) - 2.0 * (2.0 * pair + parity - 2.0) + 4.0
    offset = jnp.where(snap == snap_in, offset, -1.0)
    upper, lower = split(pick_taps(taps_ref, 0, offset))
    width = batch * rows
    rows_ref[:, 0:width] = upper
    rows_ref[:, width : 2 * width] = upper
    rows_ref[:, 2 * width :] = lower

    def halo_copy(number, side):
        fields = pl.ds(number * GROUP, GROUP)
        return pltpu.make_async_remote_copy(
            src_ref=halo_out.at[side, fields],
            dst_ref=halo_in.at[1 - side, fields],
            send_sem=halo_send.at[number, side],
            recv_sem=halo_recv.at[number, 1 - side],
            device_id=(me, low if side == 0 else high),
            device_id_type=MESH,
        )

    def part_copy(number, step, first, size):
        fields = pl.ds(number * GROUP, GROUP)
        target = lax.rem(me + step, n_sec)
        return pltpu.make_async_remote_copy(
            src_ref=own_ref.at[fields, pl.ds(first, size), target],
            dst_ref=all_ref.at[fields, pl.ds(first, size), me],
            send_sem=part_send.at[number, step - 1],
            recv_sem=part_recv.at[number, step - 1],
            device_id=(target, brick),
            device_id_type=MESH,
        )

    def is_first(step):
        return (lax.rem(me + step, n_sec) == 0).astype(jnp.int32)

    def filtered(fields, values):
        inner = []
        for value in values:
            upper, lower = split(value.reshape(snaps * rows, cells))
            inner.append(fast(jnp.concatenate([upper, lower, upper], axis=1), cross_ref[...]))
        half = groups * batch
        results = []
        for value in inner:
            upper, lower = split(value)
            blocks = []
            for start in range(0, snaps * rows, width):
                high_part, low_part = upper[start : start + width], lower[start : start + width]
                outer = fast(rows_ref[...], jnp.concatenate([high_part, low_part, high_part], axis=0))
                joined = jnp.concatenate([outer[:half], outer[half:]], axis=1)
                blocks.append(joined.reshape(groups, batch, 2 * reduced))
            results.append(jnp.concatenate(blocks, axis=1))
        if fields[0] == 0:
            pl.semaphore_wait(barrier, len(near) + n_sec - 1)
        for field, joined in zip(fields, results):
            halo_out[0, field] = joined[0].astype(BF16)
            halo_out[1, field] = joined[groups - 1].astype(BF16)
            edge_ref[field, 0] = joined[1]
            edge_ref[field, 1] = joined[groups - 2]
            for group in range(1, groups - 3):
                own_ref[field, group // n_sec, group % n_sec] = joined[group + 1].astype(BF16)
        number = fields[0] // GROUP
        halo_copy(number, 0).start()
        halo_copy(number, 1).start()
        if held > 1:
            for step in range(1, n_sec):
                part_copy(number, step, is_first(step), held - 1).start()

    def finish(number):
        fields = range(number * GROUP, (number + 1) * GROUP)
        halo_copy(number, 1).wait_recv()
        halo_copy(number, 0).wait_recv()
        for field in fields:
            own_ref[field, 0, 0] = (edge_ref[field, 0] + halo_in[0, field].astype(F32)).astype(BF16)
            own_ref[field, held - 1, n_sec - 1] = (
                edge_ref[field, 1] + halo_in[1, field].astype(F32)
            ).astype(BF16)
        for step in range(1, n_sec):
            part_copy(number, step, (held - 1) * (1 - is_first(step)), 1).start()
        for field in fields:
            for piece in range(held):
                all_ref[field, piece, me] = own_ref[field, piece, me]

    for copy in loads:
        copy.wait()

    def source(field):
        if field < 3:
            return field_ref[field]
        number = field - 3
        one = number // 3 + number // 5
        two = number - 3 * one + one * (one - 1) // 2 + one
        return field_ref[one] * field_ref[two]

    for number in range(FIELDS // GROUP):
        fields = list(range(number * GROUP, (number + 1) * GROUP))
        filtered(fields, [source(field) for field in fields])
        if number > 0:
            finish(number - 1)
    finish(FIELDS // GROUP - 1)

    count = n_sec * snaps
    gram = jnp.zeros((count, count), F32)
    for field in range(FIELDS):
        if field % GROUP == 0:
            for step in range(1, n_sec):
                part_copy(field // GROUP, step, 0, held).wait_recv()
        for piece in range(held):
            block = all_ref[field, piece].reshape(count, 2 * reduced)
            gram = gram + fast(block, block, ((1,), (1,)))

    half = count // 4
    gram_out[0] = jnp.concatenate([gram[:half], gram[half : 2 * half]], axis=1)
    gram_out[1] = jnp.concatenate([gram[2 * half : 3 * half], gram[3 * half :]], axis=1)
    copies = []

    def send(source, landing, sender, receiver, device):
        copy = pltpu.make_async_remote_copy(
            src_ref=source, dst_ref=landing, send_sem=sender, recv_sem=receiver,
            device_id=device, device_id_type=MESH,
        )
        copy.start()
        copies.append(copy)
        return copy

    send(
        gram_out.at[1 - core], core_in, core_send.at[0], core_recv.at[0], (me, partner)
    ).wait_recv()
    total = gram_out[core] + core_in[...]
    offset = 0
    for digit, peers in stages:
        z_in[offset + digit] = total
        landed = [
            send(
                z_in.at[offset + digit], z_in.at[offset + digit],
                z_send.at[offset + step], z_recv.at[offset + step], (me, peer),
            )
            for step, peer in enumerate(peers)
        ]
        for copy in landed:
            copy.wait_recv()
        total = z_in[offset]
        for slot in range(1, len(peers) + 1):
            total = total + z_in[offset + slot]
        offset += len(peers) + 1
    sec_in[me] = total
    landed = [
        send(
            sec_in.at[me], sec_in.at[me], sec_send.at[step - 1], sec_recv.at[step - 1],
            (lax.rem(me + step, n_sec), brick),
        )
        for step in range(1, n_sec)
    ]
    for copy in landed:
        copy.wait_recv()
    total = sec_in[0]
    for slot in range(1, n_sec):
        total = total + sec_in[slot]
    total_ref[core] = total
    send(
        total_ref.at[core], total_ref.at[core], core_send.at[1], core_recv.at[1], (me, partner)
    ).wait_recv()
    first, second = total_ref[0], total_ref[1]
    gram = jnp.concatenate(
        [first[:, :count], first[:, count:], second[:, :count], second[:, count:]], axis=0
    )

    weights, covariance = merge_tree(
        gram, [wide_ref[0], wide_ref[1]], [start_ref[0], start_ref[1]]
    )
    pack = sent_ref.shape[2] // share
    weights = jnp.concatenate([weights] * (pack * count // LANES), axis=1)
    weights = jnp.concatenate(
        [weights[part : part + share] for part in range(0, snaps, share) for _ in range(pack)], axis=0
    )
    row = lax.broadcasted_iota(jnp.int32, weights.shape, 0)
    lane = lax.broadcasted_iota(jnp.int32, weights.shape, 1)
    weights = jnp.where(lax.rem(row // share, pack) == lane // count, weights, 0.0)
    upper, lower = split(weights)
    weights = jnp.concatenate([upper, lower], axis=0)
    shape = (share, snaps)
    pick = (
        lax.broadcasted_iota(jnp.int32, shape, 1)
        == lax.broadcasted_iota(jnp.int32, shape, 0) + me * share
    ).astype(F32)
    energy_ref[...] = exact(pick, covariance) / total_values

    outs = []
    places = [(field, piece) for field in range(FIELDS) for piece in range(held)]
    chunks = [places[first : first + pack] for first in range(0, len(places), pack)]
    sent = 0
    for number, chunk in enumerate(chunks):
        blocks = jnp.concatenate(
            [all_ref[field, piece].reshape(count, 2 * reduced) for field, piece in chunk], axis=0
        )
        values = fast(weights[:, : len(chunk) * count], blocks)
        values = (values[: snaps * pack] + values[snaps * pack :]).astype(BF16)
        for part in range(n_sec):
            sent_ref[part, number] = values[part * share * pack : (part + 1) * share * pack]
        if number + 1 not in (len(chunks) // 2, len(chunks)):
            continue
        ready = pl.ds(sent, number + 1 - sent)
        for step in range(1, n_sec):
            target = lax.rem(me + step, n_sec)
            slot = step - 1 + (n_sec - 1) * (number + 1 == len(chunks))
            outs.append(
                send(
                    sent_ref.at[target, ready], land_ref.at[me, ready],
                    out_send.at[slot], out_recv.at[slot], (target, brick),
                )
            )
        sent = number + 1
    land_ref[me] = sent_ref[me]

    for number in range(FIELDS // GROUP):
        for side in range(2):
            halo_copy(number, side).wait_send()
        for step in range(1, n_sec):
            part_copy(number, step, 0, held).wait_send()

    for copy in outs:
        copy.wait_recv()
    for copy in copies:
        copy.wait_send()


def widen(held, land_ref, energy_ref, out_ref, result_ref):
    n_sec, chunks, rows, width = land_ref.shape
    share = out_ref.shape[1]
    pack = rows // share
    for number in range(chunks):
        for source in range(n_sec):
            values = land_ref[source, number].astype(F32)
            for part in range(min(pack, FIELDS * held - number * pack)):
                field, piece = divmod(number * pack + part, held)
                column = (piece * n_sec + source) * width
                out_ref[field, :, column : column + width] = values[part * share : (part + 1) * share]
    result_ref[...] = energy_ref[...]


def per_device(n_sec, n_brick, velocity, filter_taps, start_vectors):
    _, snaps, rows, cells = velocity.shape
    reduced = cells // 4
    groups = rows // 4 + 2
    share = snaps // n_sec
    held = rows // 4 // n_sec
    slots = max(sum(radix for _, radix in radices(n_brick // 2)), 1)
    sets = FIELDS // GROUP
    count = n_sec * snaps
    batch = max(1, min(snaps, 256 // rows))
    total_values = n_sec * snaps * FIELDS * (rows // 2) * reduced * n_brick
    width = 2 * reduced
    dma = pltpu.SemaphoreType.DMA
    pack = max(1, 256 // count)
    chunks = -(-FIELDS * held // pack)
    landed, energies = pl.pallas_call(
        functools.partial(kernel, n_sec, n_brick, total_values),
        out_shape=(
            pltpu.VMEM((n_sec, chunks, pack * share, width), BF16),
            pltpu.VMEM((share, snaps), F32),
        ),
        in_specs=[
            pl.BlockSpec(memory_space=pl.ANY),
            pl.BlockSpec(memory_space=pltpu.SMEM),
            pl.BlockSpec(memory_space=pltpu.VMEM),
        ],
        out_specs=(
            pl.BlockSpec(memory_space=pltpu.VMEM),
            pl.BlockSpec(memory_space=pltpu.VMEM),
        ),
        scratch_shapes=[
            pltpu.VMEM((3, snaps, rows, cells), F32),
            pltpu.VMEM((3 * cells, reduced), BF16),
            pltpu.VMEM((2 * groups * batch, 3 * batch * rows), BF16),
            pltpu.VMEM((FIELDS, 2, snaps, width), F32),
            pltpu.VMEM((2, FIELDS, snaps, width), BF16),
            pltpu.VMEM((2, FIELDS, snaps, width), BF16),
            pltpu.VMEM((FIELDS, held, n_sec, snaps, width), BF16),
            pltpu.VMEM((FIELDS, held, n_sec, snaps, width), BF16),
            pltpu.VMEM((2, 2 * snaps, LANES), F32),
            pltpu.VMEM((2, count // 4, 2 * count), F32),
            pltpu.VMEM((count // 4, 2 * count), F32),
            pltpu.VMEM((slots, count // 4, 2 * count), F32),
            pltpu.VMEM((n_sec, count // 4, 2 * count), F32),
            pltpu.VMEM((2, count // 4, 2 * count), F32),
            pltpu.VMEM((n_sec, chunks, pack * share, width), BF16),
            dma((3,)),
            dma((sets, 2)),
            dma((sets, 2)),
            dma((sets, n_sec - 1)),
            dma((sets, n_sec - 1)),
            dma((2,)),
            dma((2,)),
            dma((slots,)),
            dma((slots,)),
            dma((n_sec - 1,)),
            dma((n_sec - 1,)),
            dma((2 * (n_sec - 1),)),
            dma((2 * (n_sec - 1),)),
        ],
        compiler_params=pltpu.CompilerParams(
            collective_id=0, has_side_effects=True, vmem_limit_bytes=60 * 1024 * 1024
        ),
    )(velocity, filter_taps, jnp.transpose(start_vectors, (0, 2, 1)))
    basis, energies = pl.pallas_call(
        functools.partial(widen, held),
        out_shape=(
            jax.ShapeDtypeStruct((FIELDS, share, rows // 2 * reduced), F32),
            jax.ShapeDtypeStruct((share, snaps), F32),
        ),
        in_specs=[pl.BlockSpec(memory_space=pltpu.VMEM)] * 2,
        out_specs=(pl.BlockSpec(memory_space=pltpu.VMEM),) * 2,
        compiler_params=pltpu.CompilerParams(vmem_limit_bytes=8 * 1024 * 1024),
    )(landed, energies)
    return jnp.transpose(basis, (1, 0, 2)), energies


def solution(mesh):
    in_specs = (P(None, "sec", "brick", None), P(), P())
    out_specs = (P("sec", None, "brick"), P("sec", None))
    return jax.shard_map(
        functools.partial(per_device, mesh.shape["sec"], mesh.shape["brick"]),
        mesh=mesh, in_specs=in_specs, out_specs=out_specs, check_vma=False,
    )
```

```python
import functools

import jax
import jax.numpy as jnp
from jax import lax
from jax.experimental import pallas as pl
from jax.experimental.pallas import tpu as pltpu
from jax.sharding import PartitionSpec as P

CY = 32
CZ = 24
NS_STEPS = 8
TAPS = 9
FIELDS = 9
GROUP = 3
LANES = 128
MESH = pl.DeviceIdType.MESH
F32 = jnp.float32
BF16 = jnp.bfloat16


def exact(a, b, dims=((1,), (0,))):
    return lax.dot_general(
        a, b, (dims, ((), ())), precision=lax.Precision.HIGHEST, preferred_element_type=F32
    )


def fast(a, b, dims=((1,), (0,))):
    return lax.dot_general(a, b, (dims, ((), ())), preferred_element_type=F32)


def split(value):
    high = value.astype(BF16)
    return high, (value - high.astype(F32)).astype(BF16)


def grid_of(shape, dim):
    return lax.broadcasted_iota(jnp.int32, shape, dim).astype(F32)


def eye_of(size):
    shape = (size, size)
    return (
        lax.broadcasted_iota(jnp.int32, shape, 0) == lax.broadcasted_iota(jnp.int32, shape, 1)
    ).astype(F32)


def trace_of(matrix):
    return jnp.sum(matrix * eye_of(matrix.shape[0]), keepdims=True)


def pick_taps(taps_ref, dim, offset):
    total = jnp.zeros_like(offset)
    for tap in range(TAPS):
        total = jnp.where(offset == float(tap), taps_ref[dim, tap], total)
    return total


def radices(size):
    result, stride = [], 1
    while size > 1:
        radix = 4 if size % 4 == 0 else 2
        result.append((stride, radix))
        stride, size = stride * radix, size // radix
    return result


def terms(value):
    first = value.astype(BF16)
    rest = value - first.astype(F32)
    second = rest.astype(BF16)
    last = rest - second.astype(F32)
    return first, second, last.astype(BF16), rest, last


def as_left(value, order):
    slot = lax.broadcasted_iota(jnp.int32, value.shape, 1) // order
    _, _, _, rest, last = terms(value)
    return jnp.where(slot < 3, value, jnp.where(slot < 5, rest, last)).astype(BF16)


def as_right(value):
    first, second, third, _, _ = terms(value)
    blocks = [first, second, third, first, second, first]
    blank = jnp.zeros_like(first)
    spare = LANES // value.shape[0] - len(blocks)
    return jnp.concatenate(blocks + [blank] * spare, axis=0)


def narrow(left, right):
    return fast(as_left(left, right.shape[0]), as_right(right))


def newton_factors(matrices, scales):
    order = matrices[0].shape[0]
    shape = (order, LANES)
    unit = (
        lax.broadcasted_iota(jnp.int32, shape, 0)
        == lax.rem(lax.broadcasted_iota(jnp.int32, shape, 1), order)
    ).astype(F32)
    gaps = [unit - m / s for m, s in zip(matrices, scales)]
    factors = [unit + 0.5 * v for v in gaps]
    products = factors
    for step in range(NS_STEPS - 1):
        squares = [narrow(v, v) for v in gaps]
        gaps = [narrow(w, 0.75 * unit + 0.25 * v) for w, v in zip(squares, gaps)]
        factors = [unit + 0.5 * v for v in gaps]
        if step < NS_STEPS - 2:
            products = [narrow(z, e) for z, e in zip(products, factors)]
    return [(z, e, 1.0 / jnp.sqrt(s)) for z, e, s in zip(products, factors, scales)]


def times_root(value, root):
    product, factor, scale = root
    return narrow(narrow(value, product) * scale, factor)


def root_times(value, root):
    product, factor, scale = root
    return narrow(factor, narrow(product, value) * scale)


def total_of(value, copies):
    total = jnp.sum(jnp.sum(value, axis=0, keepdims=True), axis=1, keepdims=True)
    return total * (1.0 / copies)


def merge_bases(grams, wides, start, start_t):
    size = grams[0].shape[0]
    copies = LANES // start_t.shape[0]
    traces = [trace_of(g) for g in grams]
    shares = [1.0 / t for t in traces]
    basis = [exact(g, start) * s for g, s in zip(grams, shares)]
    basis_t = [exact(start_t, w) * s for w, s in zip(wides, shares)]
    for repeat in range(2):
        metric = [exact(t[:, :size], b) for t, b in zip(basis_t, basis)]
        scales = [total_of(b * b, copies) for b in basis]
        image = [exact(g, b) * s for g, b, s in zip(grams, basis, shares)]
        image_t = [exact(t[:, :size], w) * s for t, w, s in zip(basis_t, wides, shares)]
        roots = newton_factors(metric, scales)
        if repeat == 0:
            basis = [times_root(b, r) for b, r in zip(image, roots)]
            basis_t = [root_times(t, r) for t, r in zip(image_t, roots)]
    basis = [times_root(b, r) for b, r in zip(basis, roots)]
    basis_t = [root_times(t, r) for t, r in zip(basis_t, roots)]
    image = [times_root(b, r) for b, r in zip(image, roots)]
    image_t = [root_times(t, r) for t, r in zip(image_t, roots)]
    metric = [exact(t[:, :size], b) for t, b in zip(basis_t, image)]
    scales = [total_of(q * b, copies) for q, b in zip(basis, image)]
    roots = newton_factors(metric, scales)
    project = [times_root(q, r) for q, r in zip(basis, roots)]
    project_t = [root_times(t, r) for t, r in zip(basis_t, roots)]
    image = [times_root(b, r) for b, r in zip(image, roots)]
    image_t = [root_times(t, r) for t, r in zip(image_t, roots)]
    metric = [exact(t[:, :size], b) for t, b in zip(image_t, image)]
    scales = [total_of(b * b, copies) for b in image]
    spread = [narrow(p, m) for p, m in zip(project, metric)]
    spread_t = [narrow(m, t) for t, m in zip(project_t, metric)]
    roots = newton_factors(metric, scales)
    coeffs = [times_root(p, r) for p, r in zip(spread, roots)]
    coeffs_t = [root_times(t, r) for t, r in zip(spread_t, roots)]
    covariance = [m * t for m, t in zip(metric, traces)]
    return coeffs, coeffs_t, covariance


def merge_tree(gram, starts, starts_t):
    order, size = starts_t[0].shape
    columns = [gram[:, part : part + size] for part in range(0, gram.shape[0], size)]
    grams = [column[part * size : (part + 1) * size] for part, column in enumerate(columns)]
    wides = [jnp.concatenate([g] * (LANES // size), axis=1) for g in grams]
    lower, lower_t, _ = merge_bases(grams, wides, starts[0], starts_t[0])
    images = [exact(column, basis) for column, basis in zip(columns, lower)]
    lane = lax.broadcasted_iota(jnp.int32, (order, LANES), 1)
    own = lax.rem(lane, size) < order
    rows = []
    for part, basis_t in enumerate(lower_t):
        left, right = [
            exact(basis_t[:, :size], image[part * size : (part + 1) * size]) for image in images
        ]
        rows.append(jnp.where(own, left, right))
    wide = jnp.concatenate(rows, axis=0)
    (_,), (coeffs_t,), (covariance,) = merge_bases([wide[:, :size]], [wide], starts[1], starts_t[1])
    joined = jnp.concatenate(
        [
            jnp.where(lax.rem(lane // size, len(lower_t)) == part, basis_t, 0.0)
            for part, basis_t in enumerate(lower_t)
        ],
        axis=0,
    )
    return exact(coeffs_t[:, :size], joined), covariance[:, :order]


def kernel(
    n_sec, n_brick, total_values,
    velocity_ref, taps_ref, start_ref,
    land_ref, energy_ref,
    field_ref, cross_ref, rows_ref, edge_ref, halo_out, halo_in, own_ref, all_ref,
    wide_ref, gram_out, core_in, z_in, sec_in, total_ref, sent_ref,
    load_sem, halo_send, halo_recv, part_send, part_recv,
    core_send, core_recv, z_send, z_recv, sec_send, sec_recv, out_send, out_recv,
):
    snaps, rows = velocity_ref.shape[1], velocity_ref.shape[2]
    cells = velocity_ref.shape[3]
    reduced = cells // 4
    groups = rows // 4 + 2
    batch = rows_ref.shape[0] // (2 * groups)
    share = snaps // n_sec
    held = own_ref.shape[1]
    me = lax.axis_index("sec")
    brick = lax.axis_index("brick")
    low = lax.rem(brick + n_brick - 1, n_brick)
    high = lax.rem(brick + 1, n_brick)
    core = lax.rem(brick, 2)
    partner = brick + 1 - 2 * core
    stages = []
    for stride, radix in radices(n_brick // 2):
        digit = lax.rem(brick // (2 * stride), radix)
        peers = [
            brick + 2 * stride * (lax.rem(digit + step, radix) - digit) for step in range(1, radix)
        ]
        stages.append((digit, peers))
    near = [low, high] + [peer for _, peers in stages for peer in peers]

    loads = []
    for number in range(3):
        copy = pltpu.make_async_copy(
            velocity_ref.at[number], field_ref.at[number], load_sem.at[number]
        )
        copy.start()
        loads.append(copy)

    barrier = pltpu.get_barrier_semaphore()
    for target in near:
        pl.semaphore_signal(barrier, inc=1, device_id=(me, target), device_id_type=MESH)
    for step in range(1, n_sec):
        pl.semaphore_signal(
            barrier, inc=1, device_id=(lax.rem(me + step, n_sec), brick), device_id_type=MESH
        )

    for level in range(2):
        wide_ref[level] = jnp.concatenate([start_ref[level].T] * (LANES // snaps), axis=1)

    shape = (CY, reduced)
    y, point = grid_of(shape, 0), grid_of(shape, 1)
    j = jnp.floor((point + 0.5) * (2.0 / CZ))
    off_y = y - 2.0 * j + 4.0
    off_y = jnp.where(off_y < 0.0, off_y + CY, off_y)
    off_y = jnp.where(off_y >= CY, off_y - CY, off_y)
    along_y = pick_taps(taps_ref, 1, off_y)
    shape = (CZ, reduced)
    z, point = grid_of(shape, 0), grid_of(shape, 1)
    k = point - jnp.floor((point + 0.5) * (2.0 / CZ)) * (CZ // 2)
    off_z = z - 2.0 * k + 4.0
    off_z = jnp.where(off_z < 0.0, off_z + CZ, off_z)
    off_z = jnp.where(off_z >= CZ, off_z - CZ, off_z)
    along_z = pick_taps(taps_ref, 2, off_z)
    for pair in range(0, CY, 2):
        upper, lower = split(
            jnp.concatenate([along_y[row : row + 1] * along_z for row in (pair, pair + 1)], axis=0)
        )
        place = pair * CZ
        cross_ref[place : place + 2 * CZ, :] = upper
        cross_ref[cells + place : cells + place + 2 * CZ, :] = upper
        cross_ref[2 * cells + place : 2 * cells + place + 2 * CZ, :] = lower

    shape = (2 * groups * batch, batch * rows)
    target, source = grid_of(shape, 0), grid_of(shape, 1)
    parity = (target >= groups * batch).astype(F32)
    rest = target - parity * (groups * batch)
    pair = jnp.floor((rest + 0.5) * (1.0 / batch))
    snap = rest - pair * batch
    snap_in = jnp.floor((source + 0.5) * (1.0 / rows))
    offset = (source - snap_in * rows) - 2.0 * (2.0 * pair + parity - 2.0) + 4.0
    offset = jnp.where(snap == snap_in, offset, -1.0)
    upper, lower = split(pick_taps(taps_ref, 0, offset))
    width = batch * rows
    rows_ref[:, 0:width] = upper
    rows_ref[:, width : 2 * width] = upper
    rows_ref[:, 2 * width :] = lower

    def halo_copy(number, side):
        fields = pl.ds(number * GROUP, GROUP)
        return pltpu.make_async_remote_copy(
            src_ref=halo_out.at[side, fields],
            dst_ref=halo_in.at[1 - side, fields],
            send_sem=halo_send.at[number, side],
            recv_sem=halo_recv.at[number, 1 - side],
            device_id=(me, low if side == 0 else high),
            device_id_type=MESH,
        )

    def part_copy(number, step, first, size):
        fields = pl.ds(number * GROUP, GROUP)
        target = lax.rem(me + step, n_sec)
        return pltpu.make_async_remote_copy(
            src_ref=own_ref.at[fields, pl.ds(first, size), target],
            dst_ref=all_ref.at[fields, pl.ds(first, size), me],
            send_sem=part_send.at[number, step - 1],
            recv_sem=part_recv.at[number, step - 1],
            device_id=(target, brick),
            device_id_type=MESH,
        )

    def is_first(step):
        return (lax.rem(me + step, n_sec) == 0).astype(jnp.int32)

    def filtered(number, values, first=False):
        fields = [number * GROUP + place for place in range(GROUP)]
        inner = []
        for place in range(GROUP):
            upper, lower = split(values(place).reshape(snaps * rows, cells))
            inner.append(fast(jnp.concatenate([upper, lower, upper], axis=1), cross_ref[...]))
        half = groups * batch
        results = []
        for value in inner:
            upper, lower = split(value)
            blocks = []
            for start in range(0, snaps * rows, width):
                high_part, low_part = upper[start : start + width], lower[start : start + width]
                outer = fast(rows_ref[...], jnp.concatenate([high_part, low_part, high_part], axis=0))
                joined = jnp.concatenate([outer[:half], outer[half:]], axis=1)
                blocks.append(joined.reshape(groups, batch, 2 * reduced))
            results.append(jnp.concatenate(blocks, axis=1))
        if first:
            pl.semaphore_wait(barrier, len(near) + n_sec - 1)
        for field, joined in zip(fields, results):
            halo_out[0, field] = joined[0].astype(BF16)
            halo_out[1, field] = joined[groups - 1].astype(BF16)
            edge_ref[field, 0] = joined[1]
            edge_ref[field, 1] = joined[groups - 2]
            for group in range(1, groups - 3):
                own_ref[field, group // n_sec, group % n_sec] = joined[group + 1].astype(BF16)
        halo_copy(number, 0).start()
        halo_copy(number, 1).start()
        if held > 1:
            for step in range(1, n_sec):
                part_copy(number, step, is_first(step), held - 1).start()

    def finish(number):
        fields = [number * GROUP + place for place in range(GROUP)]
        halo_copy(number, 1).wait_recv()
        halo_copy(number, 0).wait_recv()
        for field in fields:
            own_ref[field, 0, 0] = (edge_ref[field, 0] + halo_in[0, field].astype(F32)).astype(BF16)
            own_ref[field, held - 1, n_sec - 1] = (
                edge_ref[field, 1] + halo_in[1, field].astype(F32)
            ).astype(BF16)
        for step in range(1, n_sec):
            part_copy(number, step, (held - 1) * (1 - is_first(step)), 1).start()
        for field in fields:
            for piece in range(held):
                all_ref[field, piece, me] = own_ref[field, piece, me]


    def source(number):
        one = number // 3 + number // 5
        two = number - 3 * one + one * (one - 1) // 2 + one
        return field_ref[one] * field_ref[two]

    def component(number):
        loads[number].wait()
        return field_ref[number]

    filtered(0, component, True)

    def step_on(number, carry):
        filtered(number, lambda place: source((number - 1) * GROUP + place))
        finish(number - 1)
        return carry

    lax.fori_loop(1, FIELDS // GROUP, step_on, 0)
    finish(FIELDS // GROUP - 1)

    count = n_sec * snaps
    gram = jnp.zeros((count, count), F32)
    for field in range(FIELDS):
        if field % GROUP == 0:
            for step in range(1, n_sec):
                part_copy(field // GROUP, step, 0, held).wait_recv()
        for piece in range(held):
            block = all_ref[field, piece].reshape(count, 2 * reduced)
            gram = gram + fast(block, block, ((1,), (1,)))

    half = count // 4
    gram_out[0] = jnp.concatenate([gram[:half], gram[half : 2 * half]], axis=1)
    gram_out[1] = jnp.concatenate([gram[2 * half : 3 * half], gram[3 * half :]], axis=1)
    copies = []

    def send(source, landing, sender, receiver, device):
        copy = pltpu.make_async_remote_copy(
            src_ref=source, dst_ref=landing, send_sem=sender, recv_sem=receiver,
            device_id=device, device_id_type=MESH,
        )
        copy.start()
        copies.append(copy)
        return copy

    send(
        gram_out.at[1 - core], core_in, core_send.at[0], core_recv.at[0], (me, partner)
    ).wait_recv()
    total = gram_out[core] + core_in[...]
    offset = 0
    for digit, peers in stages:
        z_in[offset + digit] = total
        landed = [
            send(
                z_in.at[offset + digit], z_in.at[offset + digit],
                z_send.at[offset + step], z_recv.at[offset + step], (me, peer),
            )
            for step, peer in enumerate(peers)
        ]
        for copy in landed:
            copy.wait_recv()
        total = z_in[offset]
        for slot in range(1, len(peers) + 1):
            total = total + z_in[offset + slot]
        offset += len(peers) + 1
    sec_in[me] = total
    landed = [
        send(
            sec_in.at[me], sec_in.at[me], sec_send.at[step - 1], sec_recv.at[step - 1],
            (lax.rem(me + step, n_sec), brick),
        )
        for step in range(1, n_sec)
    ]
    for copy in landed:
        copy.wait_recv()
    total = sec_in[0]
    for slot in range(1, n_sec):
        total = total + sec_in[slot]
    total_ref[core] = total
    send(
        total_ref.at[core], total_ref.at[core], core_send.at[1], core_recv.at[1], (me, partner)
    ).wait_recv()
    first, second = total_ref[0], total_ref[1]
    gram = jnp.concatenate(
        [first[:, :count], first[:, count:], second[:, :count], second[:, count:]], axis=0
    )

    weights, covariance = merge_tree(
        gram, [wide_ref[0], wide_ref[1]], [start_ref[0], start_ref[1]]
    )
    pack = sent_ref.shape[2] // share
    weights = jnp.concatenate([weights] * (pack * count // LANES), axis=1)
    weights = jnp.concatenate(
        [weights[part : part + share] for part in range(0, snaps, share) for _ in range(pack)], axis=0
    )
    row = lax.broadcasted_iota(jnp.int32, weights.shape, 0)
    lane = lax.broadcasted_iota(jnp.int32, weights.shape, 1)
    weights = jnp.where(lax.rem(row // share, pack) == lane // count, weights, 0.0)
    upper, lower = split(weights)
    weights = jnp.concatenate([upper, lower], axis=0)
    shape = (share, snaps)
    pick = (
        lax.broadcasted_iota(jnp.int32, shape, 1)
        == lax.broadcasted_iota(jnp.int32, shape, 0) + me * share
    ).astype(F32)
    energy_ref[...] = exact(pick, covariance) / total_values

    outs = []
    places = [(field, piece) for field in range(FIELDS) for piece in range(held)]
    chunks = [places[first : first + pack] for first in range(0, len(places), pack)]
    sent = 0
    for number, chunk in enumerate(chunks):
        blocks = jnp.concatenate(
            [all_ref[field, piece].reshape(count, 2 * reduced) for field, piece in chunk], axis=0
        )
        values = fast(weights[:, : len(chunk) * count], blocks)
        values = (values[: snaps * pack] + values[snaps * pack :]).astype(BF16)
        for part in range(n_sec):
            sent_ref[part, number] = values[part * share * pack : (part + 1) * share * pack]
        if number + 1 not in (len(chunks) // 2, len(chunks)):
            continue
        ready = pl.ds(sent, number + 1 - sent)
        for step in range(1, n_sec):
            target = lax.rem(me + step, n_sec)
            slot = step - 1 + (n_sec - 1) * (number + 1 == len(chunks))
            outs.append(
                send(
                    sent_ref.at[target, ready], land_ref.at[me, ready],
                    out_send.at[slot], out_recv.at[slot], (target, brick),
                )
            )
        sent = number + 1
    land_ref[me] = sent_ref[me]

    for number in range(FIELDS // GROUP):
        for side in range(2):
            halo_copy(number, side).wait_send()
        for step in range(1, n_sec):
            part_copy(number, step, 0, held).wait_send()

    for copy in outs:
        copy.wait_recv()
    for copy in copies:
        copy.wait_send()


def widen(held, land_ref, energy_ref, out_ref, result_ref):
    n_sec, chunks, rows, width = land_ref.shape
    share = out_ref.shape[1]
    pack = rows // share
    for number in range(chunks):
        for source in range(n_sec):
            values = land_ref[source, number].astype(F32)
            for part in range(min(pack, FIELDS * held - number * pack)):
                field, piece = divmod(number * pack + part, held)
                column = (piece * n_sec + source) * width
                out_ref[field, :, column : column + width] = values[part * share : (part + 1) * share]
    result_ref[...] = energy_ref[...]


def per_device(n_sec, n_brick, velocity, filter_taps, start_vectors):
    _, snaps, rows, cells = velocity.shape
    reduced = cells // 4
    groups = rows // 4 + 2
    share = snaps // n_sec
    held = rows // 4 // n_sec
    slots = max(sum(radix for _, radix in radices(n_brick // 2)), 1)
    sets = FIELDS // GROUP
    count = n_sec * snaps
    batch = max(1, min(snaps, 256 // rows))
    total_values = n_sec * snaps * FIELDS * (rows // 2) * reduced * n_brick
    width = 2 * reduced
    dma = pltpu.SemaphoreType.DMA
    pack = max(1, 256 // count)
    chunks = -(-FIELDS * held // pack)
    landed, energies = pl.pallas_call(
        functools.partial(kernel, n_sec, n_brick, total_values),
        out_shape=(
            pltpu.VMEM((n_sec, chunks, pack * share, width), BF16),
            pltpu.VMEM((share, snaps), F32),
        ),
        in_specs=[
            pl.BlockSpec(memory_space=pl.ANY),
            pl.BlockSpec(memory_space=pltpu.SMEM),
            pl.BlockSpec(memory_space=pltpu.VMEM),
        ],
        out_specs=(
            pl.BlockSpec(memory_space=pltpu.VMEM),
            pl.BlockSpec(memory_space=pltpu.VMEM),
        ),
        scratch_shapes=[
            pltpu.VMEM((3, snaps, rows, cells), F32),
            pltpu.VMEM((3 * cells, reduced), BF16),
            pltpu.VMEM((2 * groups * batch, 3 * batch * rows), BF16),
            pltpu.VMEM((FIELDS, 2, snaps, width), F32),
            pltpu.VMEM((2, FIELDS, snaps, width), BF16),
            pltpu.VMEM((2, FIELDS, snaps, width), BF16),
            pltpu.VMEM((FIELDS, held, n_sec, snaps, width), BF16),
            pltpu.VMEM((FIELDS, held, n_sec, snaps, width), BF16),
            pltpu.VMEM((2, 2 * snaps, LANES), F32),
            pltpu.VMEM((2, count // 4, 2 * count), F32),
            pltpu.VMEM((count // 4, 2 * count), F32),
            pltpu.VMEM((slots, count // 4, 2 * count), F32),
            pltpu.VMEM((n_sec, count // 4, 2 * count), F32),
            pltpu.VMEM((2, count // 4, 2 * count), F32),
            pltpu.VMEM((n_sec, chunks, pack * share, width), BF16),
            dma((3,)),
            dma((sets, 2)),
            dma((sets, 2)),
            dma((sets, n_sec - 1)),
            dma((sets, n_sec - 1)),
            dma((2,)),
            dma((2,)),
            dma((slots,)),
            dma((slots,)),
            dma((n_sec - 1,)),
            dma((n_sec - 1,)),
            dma((2 * (n_sec - 1),)),
            dma((2 * (n_sec - 1),)),
        ],
        compiler_params=pltpu.CompilerParams(
            collective_id=0, has_side_effects=True, vmem_limit_bytes=60 * 1024 * 1024
        ),
    )(velocity, filter_taps, jnp.transpose(start_vectors, (0, 2, 1)))
    basis, energies = pl.pallas_call(
        functools.partial(widen, held),
        out_shape=(
            jax.ShapeDtypeStruct((FIELDS, share, rows // 2 * reduced), F32),
            jax.ShapeDtypeStruct((share, snaps), F32),
        ),
        in_specs=[pl.BlockSpec(memory_space=pltpu.VMEM)] * 2,
        out_specs=(pl.BlockSpec(memory_space=pltpu.VMEM),) * 2,
        compiler_params=pltpu.CompilerParams(vmem_limit_bytes=8 * 1024 * 1024),
    )(landed, energies)
    return jnp.transpose(basis, (1, 0, 2)), energies


def solution(mesh):
    in_specs = (P(None, "sec", "brick", None), P(), P())
    out_specs = (P("sec", None, "brick"), P("sec", None))
    return jax.shard_map(
        functools.partial(per_device, mesh.shape["sec"], mesh.shape["brick"]),
        mesh=mesh, in_specs=in_specs, out_specs=out_specs, check_vma=False,
    )
```

```python
import functools

import jax
import jax.numpy as jnp
from jax import lax
from jax.experimental import pallas as pl
from jax.experimental.pallas import tpu as pltpu
from jax.sharding import PartitionSpec as P

CY = 32
CZ = 24
NS_STEPS = 8
TAPS = 9
FIELDS = 9
GROUP = 3
LANES = 128
ROOT = 3.821640164404114
MESH = pl.DeviceIdType.MESH
F32 = jnp.float32
BF16 = jnp.bfloat16


def exact(a, b, dims=((1,), (0,))):
    return lax.dot_general(
        a, b, (dims, ((), ())), precision=lax.Precision.HIGHEST, preferred_element_type=F32
    )


def fast(a, b, dims=((1,), (0,))):
    return lax.dot_general(a, b, (dims, ((), ())), preferred_element_type=F32)


def split(value):
    high = value.astype(BF16)
    return high, (value - high.astype(F32)).astype(BF16)


def grid_of(shape, dim):
    return lax.broadcasted_iota(jnp.int32, shape, dim).astype(F32)


def eye_of(size):
    shape = (size, size)
    return (
        lax.broadcasted_iota(jnp.int32, shape, 0) == lax.broadcasted_iota(jnp.int32, shape, 1)
    ).astype(F32)


def trace_of(matrix):
    return jnp.sum(matrix * eye_of(matrix.shape[0]), keepdims=True)


def pick_taps(taps_ref, dim, offset):
    total = jnp.zeros_like(offset)
    for tap in range(TAPS):
        total = jnp.where(offset == float(tap), taps_ref[dim, tap], total)
    return total


def radices(size):
    result, stride = [], 1
    while size > 1:
        radix = 4 if size % 4 == 0 else 2
        result.append((stride, radix))
        stride, size = stride * radix, size // radix
    return result


def terms(value):
    first = value.astype(BF16)
    rest = value - first.astype(F32)
    second = rest.astype(BF16)
    last = rest - second.astype(F32)
    return first, second, last.astype(BF16), rest, last


def as_left(value, order):
    slot = lax.broadcasted_iota(jnp.int32, value.shape, 1) // order
    _, _, _, rest, last = terms(value)
    return jnp.where(slot < 3, value, jnp.where(slot < 5, rest, last)).astype(BF16)


def as_right(value):
    first, second, third, _, _ = terms(value)
    blocks = [first, second, third, first, second, first]
    blank = jnp.zeros_like(first)
    spare = LANES // value.shape[0] - len(blocks)
    return jnp.concatenate(blocks + [blank] * spare, axis=0)


def narrow(left, right):
    return fast(as_left(left, right.shape[0]), as_right(right))


def square_and_apply(values, products):
    order = values[0].shape[0]
    joined = [narrow(jnp.concatenate([v, z], axis=0), v) for v, z in zip(values, products)]
    return [j[:order] for j in joined], [z + 0.5 * j[order:] for j, z in zip(joined, products)]


def newton_factors(matrices, scales):
    order = matrices[0].shape[0]
    shape = (order, LANES)
    unit = (
        lax.broadcasted_iota(jnp.int32, shape, 0)
        == lax.rem(lax.broadcasted_iota(jnp.int32, shape, 1), order)
    ).astype(F32)
    gaps = [unit - m / s for m, s in zip(matrices, scales)]
    products = None
    left = NS_STEPS - 1
    while left > 0:
        if products is None:
            squares = [narrow(v, v) for v in gaps]
            products = [unit + 0.5 * v for v in gaps]
        else:
            squares, products = square_and_apply(gaps, products)
        if left < 3 or len(gaps) > 1:
            gaps = [narrow(w, 0.75 * unit + 0.25 * v) for w, v in zip(squares, gaps)]
            left -= 1
        else:
            sums = [3.0 * v + w for w, v in zip(squares, gaps)]
            once = [narrow(w, 0.75 * unit + 0.25 * v) for w, v in zip(squares, gaps)]
            doubles = [narrow(a, a) for a in sums]
            cross = [narrow(w, a) for w, a in zip(squares, sums)]
            powers, products = square_and_apply(once, products)
            heads = [narrow(g, c) for g, c in zip(once, cross)]
            tails = [
                (1.0 / 16) * narrow(c, d) + (3.0 + ROOT) * narrow(a, g) + (3.0 * ROOT) * a
                for a, c, d, g in zip(sums, cross, doubles, once)
            ]
            twice = [narrow(p, 0.75 * unit + 0.25 * g) for p, g in zip(powers, once)]
            highs = [narrow(h, t) for h, t in zip(heads, tails)]
            lows = [
                narrow(3.0 * g + p, p + (3.0 - ROOT) * g + ROOT * (ROOT - 3.0) * unit)
                for p, g in zip(powers, once)
            ]
            gaps = [narrow(h, l) * (1.0 / 4096) for h, l in zip(highs, lows)]
            products = [narrow(z, unit + 0.5 * w) for z, w in zip(products, twice)]
            left -= 3
    factors = [unit + 0.5 * v for v in gaps]
    return [(z, e, 1.0 / jnp.sqrt(s)) for z, e, s in zip(products, factors, scales)]


def times_root(value, root):
    product, factor, scale = root
    return narrow(narrow(value, product) * scale, factor)


def root_times(value, root):
    product, factor, scale = root
    return narrow(factor, narrow(product, value) * scale)


def total_of(value, copies):
    total = jnp.sum(jnp.sum(value, axis=0, keepdims=True), axis=1, keepdims=True)
    return total * (1.0 / copies)


def merge_bases(grams, wides, start, start_t):
    size = grams[0].shape[0]
    copies = LANES // start_t.shape[0]
    traces = [trace_of(g) for g in grams]
    shares = [1.0 / t for t in traces]
    basis = [exact(g, start) * s for g, s in zip(grams, shares)]
    basis_t = [exact(start_t, w) * s for w, s in zip(wides, shares)]
    for repeat in range(2):
        metric = [exact(t[:, :size], b) for t, b in zip(basis_t, basis)]
        scales = [total_of(b * b, copies) for b in basis]
        image = [exact(g, b) * s for g, b, s in zip(grams, basis, shares)]
        image_t = [exact(t[:, :size], w) * s for t, w, s in zip(basis_t, wides, shares)]
        roots = newton_factors(metric, scales)
        if repeat == 0:
            basis = [times_root(b, r) for b, r in zip(image, roots)]
            basis_t = [root_times(t, r) for t, r in zip(image_t, roots)]
    basis = [times_root(b, r) for b, r in zip(basis, roots)]
    basis_t = [root_times(t, r) for t, r in zip(basis_t, roots)]
    image = [times_root(b, r) for b, r in zip(image, roots)]
    image_t = [root_times(t, r) for t, r in zip(image_t, roots)]
    metric = [exact(t[:, :size], b) for t, b in zip(basis_t, image)]
    scales = [total_of(q * b, copies) for q, b in zip(basis, image)]
    roots = newton_factors(metric, scales)
    project = [times_root(q, r) for q, r in zip(basis, roots)]
    project_t = [root_times(t, r) for t, r in zip(basis_t, roots)]
    image = [times_root(b, r) for b, r in zip(image, roots)]
    image_t = [root_times(t, r) for t, r in zip(image_t, roots)]
    metric = [exact(t[:, :size], b) for t, b in zip(image_t, image)]
    scales = [total_of(b * b, copies) for b in image]
    spread = [narrow(p, m) for p, m in zip(project, metric)]
    spread_t = [narrow(m, t) for t, m in zip(project_t, metric)]
    roots = newton_factors(metric, scales)
    coeffs = [times_root(p, r) for p, r in zip(spread, roots)]
    coeffs_t = [root_times(t, r) for t, r in zip(spread_t, roots)]
    covariance = [m * t for m, t in zip(metric, traces)]
    return coeffs, coeffs_t, covariance


def merge_tree(gram, starts, starts_t):
    order, size = starts_t[0].shape
    columns = [gram[:, part : part + size] for part in range(0, gram.shape[0], size)]
    grams = [column[part * size : (part + 1) * size] for part, column in enumerate(columns)]
    wides = [jnp.concatenate([g] * (LANES // size), axis=1) for g in grams]
    lower, lower_t, _ = merge_bases(grams, wides, starts[0], starts_t[0])
    images = [exact(column, basis) for column, basis in zip(columns, lower)]
    lane = lax.broadcasted_iota(jnp.int32, (order, LANES), 1)
    own = lax.rem(lane, size) < order
    rows = []
    for part, basis_t in enumerate(lower_t):
        left, right = [
            exact(basis_t[:, :size], image[part * size : (part + 1) * size]) for image in images
        ]
        rows.append(jnp.where(own, left, right))
    wide = jnp.concatenate(rows, axis=0)
    (_,), (coeffs_t,), (covariance,) = merge_bases([wide[:, :size]], [wide], starts[1], starts_t[1])
    joined = jnp.concatenate(
        [
            jnp.where(lax.rem(lane // size, len(lower_t)) == part, basis_t, 0.0)
            for part, basis_t in enumerate(lower_t)
        ],
        axis=0,
    )
    return exact(coeffs_t[:, :size], joined), covariance[:, :order]


def kernel(
    n_sec, n_brick, total_values,
    velocity_ref, taps_ref, start_ref,
    land_ref, energy_ref,
    field_ref, cross_ref, rows_ref, edge_ref, halo_out, halo_in, own_ref, all_ref,
    wide_ref, gram_out, core_in, z_in, sec_in, total_ref, sent_ref,
    load_sem, halo_send, halo_recv, part_send, part_recv,
    core_send, core_recv, z_send, z_recv, sec_send, sec_recv, out_send, out_recv,
):
    snaps, rows = velocity_ref.shape[1], velocity_ref.shape[2]
    cells = velocity_ref.shape[3]
    reduced = cells // 4
    groups = rows // 4 + 2
    batch = rows_ref.shape[0] // (2 * groups)
    share = snaps // n_sec
    held = own_ref.shape[1]
    me = lax.axis_index("sec")
    brick = lax.axis_index("brick")
    low = lax.rem(brick + n_brick - 1, n_brick)
    high = lax.rem(brick + 1, n_brick)
    core = lax.rem(brick, 2)
    partner = brick + 1 - 2 * core
    stages = []
    for stride, radix in radices(n_brick // 2):
        digit = lax.rem(brick // (2 * stride), radix)
        peers = [
            brick + 2 * stride * (lax.rem(digit + step, radix) - digit) for step in range(1, radix)
        ]
        stages.append((digit, peers))
    near = [low, high] + [peer for _, peers in stages for peer in peers]

    loads = []
    for number in range(3):
        copy = pltpu.make_async_copy(
            velocity_ref.at[number], field_ref.at[number], load_sem.at[number]
        )
        copy.start()
        loads.append(copy)

    barrier = pltpu.get_barrier_semaphore()
    for target in near:
        pl.semaphore_signal(barrier, inc=1, device_id=(me, target), device_id_type=MESH)
    for step in range(1, n_sec):
        pl.semaphore_signal(
            barrier, inc=1, device_id=(lax.rem(me + step, n_sec), brick), device_id_type=MESH
        )

    for level in range(2):
        wide_ref[level] = jnp.concatenate([start_ref[level].T] * (LANES // snaps), axis=1)

    shape = (CY, reduced)
    y, point = grid_of(shape, 0), grid_of(shape, 1)
    j = jnp.floor((point + 0.5) * (2.0 / CZ))
    off_y = y - 2.0 * j + 4.0
    off_y = jnp.where(off_y < 0.0, off_y + CY, off_y)
    off_y = jnp.where(off_y >= CY, off_y - CY, off_y)
    along_y = pick_taps(taps_ref, 1, off_y)
    shape = (CZ, reduced)
    z, point = grid_of(shape, 0), grid_of(shape, 1)
    k = point - jnp.floor((point + 0.5) * (2.0 / CZ)) * (CZ // 2)
    off_z = z - 2.0 * k + 4.0
    off_z = jnp.where(off_z < 0.0, off_z + CZ, off_z)
    off_z = jnp.where(off_z >= CZ, off_z - CZ, off_z)
    along_z = pick_taps(taps_ref, 2, off_z)
    for pair in range(0, CY, 2):
        upper, lower = split(
            jnp.concatenate([along_y[row : row + 1] * along_z for row in (pair, pair + 1)], axis=0)
        )
        place = pair * CZ
        cross_ref[place : place + 2 * CZ, :] = upper
        cross_ref[cells + place : cells + place + 2 * CZ, :] = upper
        cross_ref[2 * cells + place : 2 * cells + place + 2 * CZ, :] = lower

    shape = (2 * groups * batch, batch * rows)
    target, source = grid_of(shape, 0), grid_of(shape, 1)
    parity = (target >= groups * batch).astype(F32)
    rest = target - parity * (groups * batch)
    pair = jnp.floor((rest + 0.5) * (1.0 / batch))
    snap = rest - pair * batch
    snap_in = jnp.floor((source + 0.5) * (1.0 / rows))
    offset = (source - snap_in * rows) - 2.0 * (2.0 * pair + parity - 2.0) + 4.0
    offset = jnp.where(snap == snap_in, offset, -1.0)
    upper, lower = split(pick_taps(taps_ref, 0, offset))
    width = batch * rows
    rows_ref[:, 0:width] = upper
    rows_ref[:, width : 2 * width] = upper
    rows_ref[:, 2 * width :] = lower

    def halo_copy(number, side):
        fields = pl.ds(number * GROUP, GROUP)
        return pltpu.make_async_remote_copy(
            src_ref=halo_out.at[side, fields],
            dst_ref=halo_in.at[1 - side, fields],
            send_sem=halo_send.at[number, side],
            recv_sem=halo_recv.at[number, 1 - side],
            device_id=(me, low if side == 0 else high),
            device_id_type=MESH,
        )

    def part_copy(number, step, first, size):
        fields = pl.ds(number * GROUP, GROUP)
        target = lax.rem(me + step, n_sec)
        return pltpu.make_async_remote_copy(
            src_ref=own_ref.at[fields, pl.ds(first, size), target],
            dst_ref=all_ref.at[fields, pl.ds(first, size), me],
            send_sem=part_send.at[number, step - 1],
            recv_sem=part_recv.at[number, step - 1],
            device_id=(target, brick),
            device_id_type=MESH,
        )

    def is_first(step):
        return (lax.rem(me + step, n_sec) == 0).astype(jnp.int32)

    def filtered(number, values, first=False):
        fields = [number * GROUP + place for place in range(GROUP)]
        inner = []
        for place in range(GROUP):
            upper, lower = split(values(place).reshape(snaps * rows, cells))
            inner.append(fast(jnp.concatenate([upper, lower, upper], axis=1), cross_ref[...]))
        half = groups * batch
        results = []
        for value in inner:
            upper, lower = split(value)
            blocks = []
            for start in range(0, snaps * rows, width):
                high_part, low_part = upper[start : start + width], lower[start : start + width]
                outer = fast(rows_ref[...], jnp.concatenate([high_part, low_part, high_part], axis=0))
                joined = jnp.concatenate([outer[:half], outer[half:]], axis=1)
                blocks.append(joined.reshape(groups, batch, 2 * reduced))
            results.append(jnp.concatenate(blocks, axis=1))
        if first:
            pl.semaphore_wait(barrier, len(near) + n_sec - 1)
        for field, joined in zip(fields, results):
            halo_out[0, field] = joined[0].astype(BF16)
            halo_out[1, field] = joined[groups - 1].astype(BF16)
            edge_ref[field, 0] = joined[1]
            edge_ref[field, 1] = joined[groups - 2]
            for group in range(1, groups - 3):
                own_ref[field, group // n_sec, group % n_sec] = joined[group + 1].astype(BF16)
        halo_copy(number, 0).start()
        halo_copy(number, 1).start()
        if held > 1:
            for step in range(1, n_sec):
                part_copy(number, step, is_first(step), held - 1).start()

    def finish(number):
        fields = [number * GROUP + place for place in range(GROUP)]
        halo_copy(number, 1).wait_recv()
        halo_copy(number, 0).wait_recv()
        for field in fields:
            own_ref[field, 0, 0] = (edge_ref[field, 0] + halo_in[0, field].astype(F32)).astype(BF16)
            own_ref[field, held - 1, n_sec - 1] = (
                edge_ref[field, 1] + halo_in[1, field].astype(F32)
            ).astype(BF16)
        for step in range(1, n_sec):
            part_copy(number, step, (held - 1) * (1 - is_first(step)), 1).start()
        for field in fields:
            for piece in range(held):
                all_ref[field, piece, me] = own_ref[field, piece, me]


    def source(number):
        one = number // 3 + number // 5
        two = number - 3 * one + one * (one - 1) // 2 + one
        return field_ref[one] * field_ref[two]

    def component(number):
        loads[number].wait()
        return field_ref[number]

    filtered(0, component, True)

    def step_on(number, carry):
        filtered(number, lambda place: source((number - 1) * GROUP + place))
        finish(number - 1)
        return carry

    lax.fori_loop(1, FIELDS // GROUP, step_on, 0)
    finish(FIELDS // GROUP - 1)

    count = n_sec * snaps
    gram = jnp.zeros((count, count), F32)
    for field in range(FIELDS):
        if field % GROUP == 0:
            for step in range(1, n_sec):
                part_copy(field // GROUP, step, 0, held).wait_recv()
        for piece in range(held):
            block = all_ref[field, piece].reshape(count, 2 * reduced)
            gram = gram + fast(block, block, ((1,), (1,)))

    half = count // 4
    gram_out[0] = jnp.concatenate([gram[:half], gram[half : 2 * half]], axis=1)
    gram_out[1] = jnp.concatenate([gram[2 * half : 3 * half], gram[3 * half :]], axis=1)
    copies = []

    def send(source, landing, sender, receiver, device):
        copy = pltpu.make_async_remote_copy(
            src_ref=source, dst_ref=landing, send_sem=sender, recv_sem=receiver,
            device_id=device, device_id_type=MESH,
        )
        copy.start()
        copies.append(copy)
        return copy

    send(
        gram_out.at[1 - core], core_in, core_send.at[0], core_recv.at[0], (me, partner)
    ).wait_recv()
    total = gram_out[core] + core_in[...]
    offset = 0
    for digit, peers in stages:
        z_in[offset + digit] = total
        landed = [
            send(
                z_in.at[offset + digit], z_in.at[offset + digit],
                z_send.at[offset + step], z_recv.at[offset + step], (me, peer),
            )
            for step, peer in enumerate(peers)
        ]
        for copy in landed:
            copy.wait_recv()
        total = z_in[offset]
        for slot in range(1, len(peers) + 1):
            total = total + z_in[offset + slot]
        offset += len(peers) + 1
    sec_in[me] = total
    landed = [
        send(
            sec_in.at[me], sec_in.at[me], sec_send.at[step - 1], sec_recv.at[step - 1],
            (lax.rem(me + step, n_sec), brick),
        )
        for step in range(1, n_sec)
    ]
    for copy in landed:
        copy.wait_recv()
    total = sec_in[0]
    for slot in range(1, n_sec):
        total = total + sec_in[slot]
    total_ref[core] = total
    send(
        total_ref.at[core], total_ref.at[core], core_send.at[1], core_recv.at[1], (me, partner)
    ).wait_recv()
    first, second = total_ref[0], total_ref[1]
    gram = jnp.concatenate(
        [first[:, :count], first[:, count:], second[:, :count], second[:, count:]], axis=0
    )

    weights, covariance = merge_tree(
        gram, [wide_ref[0], wide_ref[1]], [start_ref[0], start_ref[1]]
    )
    pack = sent_ref.shape[2] // share
    weights = jnp.concatenate([weights] * (pack * count // LANES), axis=1)
    weights = jnp.concatenate(
        [weights[part : part + share] for part in range(0, snaps, share) for _ in range(pack)], axis=0
    )
    row = lax.broadcasted_iota(jnp.int32, weights.shape, 0)
    lane = lax.broadcasted_iota(jnp.int32, weights.shape, 1)
    weights = jnp.where(lax.rem(row // share, pack) == lane // count, weights, 0.0)
    upper, lower = split(weights)
    weights = jnp.concatenate([upper, lower], axis=0)
    shape = (share, snaps)
    pick = (
        lax.broadcasted_iota(jnp.int32, shape, 1)
        == lax.broadcasted_iota(jnp.int32, shape, 0) + me * share
    ).astype(F32)
    energy_ref[...] = exact(pick, covariance) / total_values

    outs = []
    places = [(field, piece) for field in range(FIELDS) for piece in range(held)]
    chunks = [places[first : first + pack] for first in range(0, len(places), pack)]
    sent = 0
    for number, chunk in enumerate(chunks):
        blocks = jnp.concatenate(
            [all_ref[field, piece].reshape(count, 2 * reduced) for field, piece in chunk], axis=0
        )
        values = fast(weights[:, : len(chunk) * count], blocks)
        values = (values[: snaps * pack] + values[snaps * pack :]).astype(BF16)
        for part in range(n_sec):
            sent_ref[part, number] = values[part * share * pack : (part + 1) * share * pack]
        if number + 1 not in (len(chunks) // 2, len(chunks)):
            continue
        ready = pl.ds(sent, number + 1 - sent)
        for step in range(1, n_sec):
            target = lax.rem(me + step, n_sec)
            slot = step - 1 + (n_sec - 1) * (number + 1 == len(chunks))
            outs.append(
                send(
                    sent_ref.at[target, ready], land_ref.at[me, ready],
                    out_send.at[slot], out_recv.at[slot], (target, brick),
                )
            )
        sent = number + 1
    land_ref[me] = sent_ref[me]

    for number in range(FIELDS // GROUP):
        for side in range(2):
            halo_copy(number, side).wait_send()
        for step in range(1, n_sec):
            part_copy(number, step, 0, held).wait_send()

    for copy in outs:
        copy.wait_recv()
    for copy in copies:
        copy.wait_send()


def widen(held, land_ref, energy_ref, out_ref, result_ref):
    n_sec, chunks, rows, width = land_ref.shape
    share = out_ref.shape[1]
    pack = rows // share
    for number in range(chunks):
        for source in range(n_sec):
            values = land_ref[source, number].astype(F32)
            for part in range(min(pack, FIELDS * held - number * pack)):
                field, piece = divmod(number * pack + part, held)
                column = (piece * n_sec + source) * width
                out_ref[field, :, column : column + width] = values[part * share : (part + 1) * share]
    result_ref[...] = energy_ref[...]


def per_device(n_sec, n_brick, velocity, filter_taps, start_vectors):
    _, snaps, rows, cells = velocity.shape
    reduced = cells // 4
    groups = rows // 4 + 2
    share = snaps // n_sec
    held = rows // 4 // n_sec
    slots = max(sum(radix for _, radix in radices(n_brick // 2)), 1)
    sets = FIELDS // GROUP
    count = n_sec * snaps
    batch = max(1, min(snaps, 256 // rows))
    total_values = n_sec * snaps * FIELDS * (rows // 2) * reduced * n_brick
    width = 2 * reduced
    dma = pltpu.SemaphoreType.DMA
    pack = max(1, 256 // count)
    chunks = -(-FIELDS * held // pack)
    landed, energies = pl.pallas_call(
        functools.partial(kernel, n_sec, n_brick, total_values),
        out_shape=(
            pltpu.VMEM((n_sec, chunks, pack * share, width), BF16),
            pltpu.VMEM((share, snaps), F32),
        ),
        in_specs=[
            pl.BlockSpec(memory_space=pl.ANY),
            pl.BlockSpec(memory_space=pltpu.SMEM),
            pl.BlockSpec(memory_space=pltpu.VMEM),
        ],
        out_specs=(
            pl.BlockSpec(memory_space=pltpu.VMEM),
            pl.BlockSpec(memory_space=pltpu.VMEM),
        ),
        scratch_shapes=[
            pltpu.VMEM((3, snaps, rows, cells), F32),
            pltpu.VMEM((3 * cells, reduced), BF16),
            pltpu.VMEM((2 * groups * batch, 3 * batch * rows), BF16),
            pltpu.VMEM((FIELDS, 2, snaps, width), F32),
            pltpu.VMEM((2, FIELDS, snaps, width), BF16),
            pltpu.VMEM((2, FIELDS, snaps, width), BF16),
            pltpu.VMEM((FIELDS, held, n_sec, snaps, width), BF16),
            pltpu.VMEM((FIELDS, held, n_sec, snaps, width), BF16),
            pltpu.VMEM((2, 2 * snaps, LANES), F32),
            pltpu.VMEM((2, count // 4, 2 * count), F32),
            pltpu.VMEM((count // 4, 2 * count), F32),
            pltpu.VMEM((slots, count // 4, 2 * count), F32),
            pltpu.VMEM((n_sec, count // 4, 2 * count), F32),
            pltpu.VMEM((2, count // 4, 2 * count), F32),
            pltpu.VMEM((n_sec, chunks, pack * share, width), BF16),
            dma((3,)),
            dma((sets, 2)),
            dma((sets, 2)),
            dma((sets, n_sec - 1)),
            dma((sets, n_sec - 1)),
            dma((2,)),
            dma((2,)),
            dma((slots,)),
            dma((slots,)),
            dma((n_sec - 1,)),
            dma((n_sec - 1,)),
            dma((2 * (n_sec - 1),)),
            dma((2 * (n_sec - 1),)),
        ],
        compiler_params=pltpu.CompilerParams(
            collective_id=0, has_side_effects=True, vmem_limit_bytes=60 * 1024 * 1024
        ),
    )(velocity, filter_taps, jnp.transpose(start_vectors, (0, 2, 1)))
    basis, energies = pl.pallas_call(
        functools.partial(widen, held),
        out_shape=(
            jax.ShapeDtypeStruct((FIELDS, share, rows // 2 * reduced), F32),
            jax.ShapeDtypeStruct((share, snaps), F32),
        ),
        in_specs=[pl.BlockSpec(memory_space=pltpu.VMEM)] * 2,
        out_specs=(pl.BlockSpec(memory_space=pltpu.VMEM),) * 2,
        compiler_params=pltpu.CompilerParams(vmem_limit_bytes=8 * 1024 * 1024),
    )(landed, energies)
    return jnp.transpose(basis, (1, 0, 2)), energies


def solution(mesh):
    in_specs = (P(None, "sec", "brick", None), P(), P())
    out_specs = (P("sec", None, "brick"), P("sec", None))
    return jax.shard_map(
        functools.partial(per_device, mesh.shape["sec"], mesh.shape["brick"]),
        mesh=mesh, in_specs=in_specs, out_specs=out_specs, check_vma=False,
    )
```

```python
import functools

import jax
import jax.numpy as jnp
from jax import lax
from jax.experimental import pallas as pl
from jax.experimental.pallas import tpu as pltpu
from jax.sharding import PartitionSpec as P

CY = 32
CZ = 24
NS_STEPS = 8
TAPS = 9
FIELDS = 9
GROUP = 3
LANES = 128
ROOT = 3.821640164404114
MESH = pl.DeviceIdType.MESH
F32 = jnp.float32
BF16 = jnp.bfloat16


def exact(a, b, dims=((1,), (0,))):
    return lax.dot_general(
        a, b, (dims, ((), ())), precision=lax.Precision.HIGHEST, preferred_element_type=F32
    )


def fast(a, b, dims=((1,), (0,))):
    return lax.dot_general(a, b, (dims, ((), ())), preferred_element_type=F32)


def split(value):
    high = value.astype(BF16)
    return high, (value - high.astype(F32)).astype(BF16)


def grid_of(shape, dim):
    return lax.broadcasted_iota(jnp.int32, shape, dim).astype(F32)


def eye_of(size):
    shape = (size, size)
    return (
        lax.broadcasted_iota(jnp.int32, shape, 0) == lax.broadcasted_iota(jnp.int32, shape, 1)
    ).astype(F32)


def trace_of(matrix):
    return jnp.sum(matrix * eye_of(matrix.shape[0]), keepdims=True)


def pick_taps(taps_ref, dim, offset):
    total = jnp.zeros_like(offset)
    for tap in range(TAPS):
        total = jnp.where(offset == float(tap), taps_ref[dim, tap], total)
    return total


def radices(size):
    result, stride = [], 1
    while size > 1:
        radix = 4 if size % 4 == 0 else 2
        result.append((stride, radix))
        stride, size = stride * radix, size // radix
    return result


def terms(value):
    first = value.astype(BF16)
    rest = value - first.astype(F32)
    second = rest.astype(BF16)
    last = rest - second.astype(F32)
    return first, second, last.astype(BF16), rest, last


def as_left(value, order):
    slot = lax.broadcasted_iota(jnp.int32, value.shape, 1) // order
    _, _, _, rest, last = terms(value)
    return jnp.where(slot < 3, value, jnp.where(slot < 5, rest, last)).astype(BF16)


def as_right(value):
    first, second, third, _, _ = terms(value)
    blocks = [first, second, third, first, second, first]
    blank = jnp.zeros_like(first)
    spare = LANES // value.shape[0] - len(blocks)
    return jnp.concatenate(blocks + [blank] * spare, axis=0)


def narrow(left, right):
    return fast(as_left(left, right.shape[0]), as_right(right))


def square_and_apply(values, products):
    order = values[0].shape[0]
    joined = [narrow(jnp.concatenate([v, z], axis=0), v) for v, z in zip(values, products)]
    return [j[:order] for j in joined], [z + 0.5 * j[order:] for j, z in zip(joined, products)]


def newton_factors(matrices, scales):
    order = matrices[0].shape[0]
    shape = (order, LANES)
    unit = (
        lax.broadcasted_iota(jnp.int32, shape, 0)
        == lax.rem(lax.broadcasted_iota(jnp.int32, shape, 1), order)
    ).astype(F32)
    gaps = [unit - m * (1.0 / s) for m, s in zip(matrices, scales)]
    products = None
    left = NS_STEPS - 1
    while left > 0:
        if products is None:
            squares = [narrow(v, v) for v in gaps]
            products = [unit + 0.5 * v for v in gaps]
        else:
            squares, products = square_and_apply(gaps, products)
        if left < 3 or len(gaps) > 1:
            gaps = [narrow(w, 0.75 * unit + 0.25 * v) for w, v in zip(squares, gaps)]
            left -= 1
        else:
            sums = [3.0 * v + w for w, v in zip(squares, gaps)]
            once = [narrow(w, 0.75 * unit + 0.25 * v) for w, v in zip(squares, gaps)]
            doubles = [narrow(a, a) for a in sums]
            cross = [narrow(w, a) for w, a in zip(squares, sums)]
            powers, products = square_and_apply(once, products)
            heads = [narrow(g, c) for g, c in zip(once, cross)]
            tails = [
                (1.0 / 16) * narrow(c, d) + (3.0 + ROOT) * narrow(a, g) + (3.0 * ROOT) * a
                for a, c, d, g in zip(sums, cross, doubles, once)
            ]
            twice = [narrow(p, 0.75 * unit + 0.25 * g) for p, g in zip(powers, once)]
            highs = [narrow(h, t) for h, t in zip(heads, tails)]
            lows = [
                narrow(3.0 * g + p, p + (3.0 - ROOT) * g + ROOT * (ROOT - 3.0) * unit)
                for p, g in zip(powers, once)
            ]
            gaps = [narrow(h, l) * (1.0 / 4096) for h, l in zip(highs, lows)]
            products = [narrow(z, unit + 0.5 * w) for z, w in zip(products, twice)]
            left -= 3
    factors = [unit + 0.5 * v for v in gaps]
    return [(z, e, 1.0 / jnp.sqrt(s)) for z, e, s in zip(products, factors, scales)]


def times_root(value, root):
    product, factor, scale = root
    return narrow(narrow(value, product) * scale, factor)


def root_times(value, root):
    product, factor, scale = root
    return narrow(factor, narrow(product, value) * scale)


def total_of(value, copies):
    total = jnp.sum(jnp.sum(value, axis=0, keepdims=True), axis=1, keepdims=True)
    return total * (1.0 / copies)


def merge_bases(grams, wides, start, start_t):
    size = grams[0].shape[0]
    copies = LANES // start_t.shape[0]
    traces = [trace_of(g) for g in grams]
    shares = [1.0 / t for t in traces]
    basis = [exact(g, start) * s for g, s in zip(grams, shares)]
    basis_t = [exact(start_t, w) * s for w, s in zip(wides, shares)]
    for repeat in range(2):
        metric = [exact(t[:, :size], b) for t, b in zip(basis_t, basis)]
        scales = [total_of(b * b, copies) for b in basis]
        image = [exact(g, b) * s for g, b, s in zip(grams, basis, shares)]
        image_t = [exact(t[:, :size], w) * s for t, w, s in zip(basis_t, wides, shares)]
        roots = newton_factors(metric, scales)
        if repeat == 0:
            basis = [times_root(b, r) for b, r in zip(image, roots)]
            basis_t = [root_times(t, r) for t, r in zip(image_t, roots)]
    basis = [times_root(b, r) for b, r in zip(basis, roots)]
    basis_t = [root_times(t, r) for t, r in zip(basis_t, roots)]
    image = [times_root(b, r) for b, r in zip(image, roots)]
    image_t = [root_times(t, r) for t, r in zip(image_t, roots)]
    metric = [exact(t[:, :size], b) for t, b in zip(basis_t, image)]
    scales = [total_of(q * b, copies) for q, b in zip(basis, image)]
    roots = newton_factors(metric, scales)
    project = [times_root(q, r) for q, r in zip(basis, roots)]
    project_t = [root_times(t, r) for t, r in zip(basis_t, roots)]
    image = [times_root(b, r) for b, r in zip(image, roots)]
    image_t = [root_times(t, r) for t, r in zip(image_t, roots)]
    metric = [exact(t[:, :size], b) for t, b in zip(image_t, image)]
    scales = [total_of(b * b, copies) for b in image]
    spread = [narrow(p, m) for p, m in zip(project, metric)]
    spread_t = [narrow(m, t) for t, m in zip(project_t, metric)]
    roots = newton_factors(metric, scales)
    coeffs = [times_root(p, r) for p, r in zip(spread, roots)]
    coeffs_t = [root_times(t, r) for t, r in zip(spread_t, roots)]
    covariance = [m * t for m, t in zip(metric, traces)]
    return coeffs, coeffs_t, covariance


def merge_tree(gram, starts, starts_t):
    order, size = starts_t[0].shape
    columns = [gram[:, part : part + size] for part in range(0, gram.shape[0], size)]
    grams = [column[part * size : (part + 1) * size] for part, column in enumerate(columns)]
    wides = [jnp.concatenate([g] * (LANES // size), axis=1) for g in grams]
    lower, lower_t, _ = merge_bases(grams, wides, starts[0], starts_t[0])
    images = [exact(column, basis) for column, basis in zip(columns, lower)]
    lane = lax.broadcasted_iota(jnp.int32, (order, LANES), 1)
    own = lax.rem(lane, size) < order
    rows = []
    for part, basis_t in enumerate(lower_t):
        left, right = [
            exact(basis_t[:, :size], image[part * size : (part + 1) * size]) for image in images
        ]
        rows.append(jnp.where(own, left, right))
    wide = jnp.concatenate(rows, axis=0)
    (_,), (coeffs_t,), (covariance,) = merge_bases([wide[:, :size]], [wide], starts[1], starts_t[1])
    joined = jnp.concatenate(
        [
            jnp.where(lax.rem(lane // size, len(lower_t)) == part, basis_t, 0.0)
            for part, basis_t in enumerate(lower_t)
        ],
        axis=0,
    )
    return exact(coeffs_t[:, :size], joined), covariance[:, :order]


def kernel(
    n_sec, n_brick, total_values,
    velocity_ref, taps_ref, start_ref,
    land_ref, energy_ref,
    field_ref, cross_ref, rows_ref, edge_ref, halo_out, halo_in, own_ref, all_ref,
    wide_ref, gram_out, core_in, z_in, sec_in, total_ref, sent_ref,
    load_sem, halo_send, halo_recv, part_send, part_recv,
    core_send, core_recv, z_send, z_recv, sec_send, sec_recv, out_send, out_recv,
):
    snaps, rows = velocity_ref.shape[1], velocity_ref.shape[2]
    cells = velocity_ref.shape[3]
    reduced = cells // 4
    groups = rows // 4 + 2
    batch = rows_ref.shape[0] // (2 * groups)
    share = snaps // n_sec
    held = own_ref.shape[1]
    me = lax.axis_index("sec")
    brick = lax.axis_index("brick")
    low = lax.rem(brick + n_brick - 1, n_brick)
    high = lax.rem(brick + 1, n_brick)
    core = lax.rem(brick, 2)
    partner = brick + 1 - 2 * core
    stages = []
    for stride, radix in radices(n_brick // 2):
        digit = lax.rem(brick // (2 * stride), radix)
        peers = [
            brick + 2 * stride * (lax.rem(digit + step, radix) - digit) for step in range(1, radix)
        ]
        stages.append((digit, peers))
    near = [low, high] + [peer for _, peers in stages for peer in peers]

    loads = []
    for number in range(3):
        copy = pltpu.make_async_copy(
            velocity_ref.at[number], field_ref.at[number], load_sem.at[number]
        )
        copy.start()
        loads.append(copy)

    barrier = pltpu.get_barrier_semaphore()
    for target in near:
        pl.semaphore_signal(barrier, inc=1, device_id=(me, target), device_id_type=MESH)
    for step in range(1, n_sec):
        pl.semaphore_signal(
            barrier, inc=1, device_id=(lax.rem(me + step, n_sec), brick), device_id_type=MESH
        )

    for level in range(2):
        wide_ref[level] = jnp.concatenate([start_ref[level].T] * (LANES // snaps), axis=1)

    shape = (CY, reduced)
    y, point = grid_of(shape, 0), grid_of(shape, 1)
    j = jnp.floor((point + 0.5) * (2.0 / CZ))
    off_y = y - 2.0 * j + 4.0
    off_y = jnp.where(off_y < 0.0, off_y + CY, off_y)
    off_y = jnp.where(off_y >= CY, off_y - CY, off_y)
    along_y = pick_taps(taps_ref, 1, off_y)
    shape = (CZ, reduced)
    z, point = grid_of(shape, 0), grid_of(shape, 1)
    k = point - jnp.floor((point + 0.5) * (2.0 / CZ)) * (CZ // 2)
    off_z = z - 2.0 * k + 4.0
    off_z = jnp.where(off_z < 0.0, off_z + CZ, off_z)
    off_z = jnp.where(off_z >= CZ, off_z - CZ, off_z)
    along_z = pick_taps(taps_ref, 2, off_z)
    for pair in range(0, CY, 2):
        upper, lower = split(
            jnp.concatenate([along_y[row : row + 1] * along_z for row in (pair, pair + 1)], axis=0)
        )
        place = pair * CZ
        cross_ref[place : place + 2 * CZ, :] = upper
        cross_ref[cells + place : cells + place + 2 * CZ, :] = upper
        cross_ref[2 * cells + place : 2 * cells + place + 2 * CZ, :] = lower

    shape = (2 * groups * batch, batch * rows)
    target, source = grid_of(shape, 0), grid_of(shape, 1)
    parity = (target >= groups * batch).astype(F32)
    rest = target - parity * (groups * batch)
    pair = jnp.floor((rest + 0.5) * (1.0 / batch))
    snap = rest - pair * batch
    snap_in = jnp.floor((source + 0.5) * (1.0 / rows))
    offset = (source - snap_in * rows) - 2.0 * (2.0 * pair + parity - 2.0) + 4.0
    offset = jnp.where(snap == snap_in, offset, -1.0)
    upper, lower = split(pick_taps(taps_ref, 0, offset))
    width = batch * rows
    rows_ref[:, 0:width] = upper
    rows_ref[:, width : 2 * width] = upper
    rows_ref[:, 2 * width :] = lower

    def halo_copy(number, side):
        fields = pl.ds(number * GROUP, GROUP)
        return pltpu.make_async_remote_copy(
            src_ref=halo_out.at[side, fields],
            dst_ref=halo_in.at[1 - side, fields],
            send_sem=halo_send.at[number, side],
            recv_sem=halo_recv.at[number, 1 - side],
            device_id=(me, low if side == 0 else high),
            device_id_type=MESH,
        )

    def part_copy(number, step, first, size):
        fields = pl.ds(number * GROUP, GROUP)
        target = lax.rem(me + step, n_sec)
        return pltpu.make_async_remote_copy(
            src_ref=own_ref.at[fields, pl.ds(first, size), target],
            dst_ref=all_ref.at[fields, pl.ds(first, size), me],
            send_sem=part_send.at[number, step - 1],
            recv_sem=part_recv.at[number, step - 1],
            device_id=(target, brick),
            device_id_type=MESH,
        )

    def is_first(step):
        return (lax.rem(me + step, n_sec) == 0).astype(jnp.int32)

    def filtered(number, values, first=False):
        fields = [number * GROUP + place for place in range(GROUP)]
        inner = []
        for place in range(GROUP):
            upper, lower = split(values(place).reshape(snaps * rows, cells))
            inner.append(fast(jnp.concatenate([upper, lower, upper], axis=1), cross_ref[...]))
        half = groups * batch
        results = []
        for value in inner:
            upper, lower = split(value)
            blocks = []
            for start in range(0, snaps * rows, width):
                high_part, low_part = upper[start : start + width], lower[start : start + width]
                outer = fast(rows_ref[...], jnp.concatenate([high_part, low_part, high_part], axis=0))
                joined = jnp.concatenate([outer[:half], outer[half:]], axis=1)
                blocks.append(joined.reshape(groups, batch, 2 * reduced))
            results.append(jnp.concatenate(blocks, axis=1))
        if first:
            pl.semaphore_wait(barrier, len(near) + n_sec - 1)
        for field, joined in zip(fields, results):
            halo_out[0, field] = joined[0].astype(BF16)
            halo_out[1, field] = joined[groups - 1].astype(BF16)
            edge_ref[field, 0] = joined[1]
            edge_ref[field, 1] = joined[groups - 2]
            for group in range(1, groups - 3):
                own_ref[field, group // n_sec, group % n_sec] = joined[group + 1].astype(BF16)
        halo_copy(number, 0).start()
        halo_copy(number, 1).start()
        if held > 1:
            for step in range(1, n_sec):
                part_copy(number, step, is_first(step), held - 1).start()

    def finish(number):
        fields = [number * GROUP + place for place in range(GROUP)]
        halo_copy(number, 1).wait_recv()
        halo_copy(number, 0).wait_recv()
        for field in fields:
            own_ref[field, 0, 0] = (edge_ref[field, 0] + halo_in[0, field].astype(F32)).astype(BF16)
            own_ref[field, held - 1, n_sec - 1] = (
                edge_ref[field, 1] + halo_in[1, field].astype(F32)
            ).astype(BF16)
        for step in range(1, n_sec):
            part_copy(number, step, (held - 1) * (1 - is_first(step)), 1).start()
        for field in fields:
            for piece in range(held):
                all_ref[field, piece, me] = own_ref[field, piece, me]


    def source(number):
        one = number // 3 + number // 5
        two = number - 3 * one + one * (one - 1) // 2 + one
        return field_ref[one] * field_ref[two]

    def component(number):
        loads[number].wait()
        return field_ref[number]

    filtered(0, component, True)

    def step_on(number, carry):
        filtered(number, lambda place: source((number - 1) * GROUP + place))
        finish(number - 1)
        return carry

    lax.fori_loop(1, FIELDS // GROUP, step_on, 0)
    finish(FIELDS // GROUP - 1)

    count = n_sec * snaps
    gram = jnp.zeros((count, count), F32)
    for field in range(FIELDS):
        if field % GROUP == 0:
            for step in range(1, n_sec):
                part_copy(field // GROUP, step, 0, held).wait_recv()
        for piece in range(held):
            block = all_ref[field, piece].reshape(count, 2 * reduced)
            gram = gram + fast(block, block, ((1,), (1,)))

    half = count // 4
    gram_out[0] = jnp.concatenate([gram[:half], gram[half : 2 * half]], axis=1)
    gram_out[1] = jnp.concatenate([gram[2 * half : 3 * half], gram[3 * half :]], axis=1)
    copies = []

    def send(source, landing, sender, receiver, device):
        copy = pltpu.make_async_remote_copy(
            src_ref=source, dst_ref=landing, send_sem=sender, recv_sem=receiver,
            device_id=device, device_id_type=MESH,
        )
        copy.start()
        copies.append(copy)
        return copy

    send(
        gram_out.at[1 - core], core_in, core_send.at[0], core_recv.at[0], (me, partner)
    ).wait_recv()
    total = gram_out[core] + core_in[...]
    offset = 0
    for digit, peers in stages:
        z_in[offset + digit] = total
        landed = [
            send(
                z_in.at[offset + digit], z_in.at[offset + digit],
                z_send.at[offset + step], z_recv.at[offset + step], (me, peer),
            )
            for step, peer in enumerate(peers)
        ]
        for copy in landed:
            copy.wait_recv()
        total = z_in[offset]
        for slot in range(1, len(peers) + 1):
            total = total + z_in[offset + slot]
        offset += len(peers) + 1
    sec_in[me] = total
    landed = [
        send(
            sec_in.at[me], sec_in.at[me], sec_send.at[step - 1], sec_recv.at[step - 1],
            (lax.rem(me + step, n_sec), brick),
        )
        for step in range(1, n_sec)
    ]
    for copy in landed:
        copy.wait_recv()
    total = sec_in[0]
    for slot in range(1, n_sec):
        total = total + sec_in[slot]
    total_ref[core] = total
    send(
        total_ref.at[core], total_ref.at[core], core_send.at[1], core_recv.at[1], (me, partner)
    ).wait_recv()
    first, second = total_ref[0], total_ref[1]
    gram = jnp.concatenate(
        [first[:, :count], first[:, count:], second[:, :count], second[:, count:]], axis=0
    )

    weights, covariance = merge_tree(
        gram, [wide_ref[0], wide_ref[1]], [start_ref[0], start_ref[1]]
    )
    pack = sent_ref.shape[2] // share
    weights = jnp.concatenate([weights] * (pack * count // LANES), axis=1)
    weights = jnp.concatenate(
        [weights[part : part + share] for part in range(0, snaps, share) for _ in range(pack)], axis=0
    )
    row = lax.broadcasted_iota(jnp.int32, weights.shape, 0)
    lane = lax.broadcasted_iota(jnp.int32, weights.shape, 1)
    weights = jnp.where(lax.rem(row // share, pack) == lane // count, weights, 0.0)
    upper, lower = split(weights)
    weights = jnp.concatenate([upper, lower], axis=0)
    outs = []
    places = [(field, piece) for field in range(FIELDS) for piece in range(held)]
    chunks = [places[first : first + pack] for first in range(0, len(places), pack)]
    sent = 0
    for number, chunk in enumerate(chunks):
        blocks = jnp.concatenate(
            [all_ref[field, piece].reshape(count, 2 * reduced) for field, piece in chunk], axis=0
        )
        values = fast(weights[:, : len(chunk) * count], blocks)
        values = (values[: snaps * pack] + values[snaps * pack :]).astype(BF16)
        for part in range(n_sec):
            sent_ref[part, number] = values[part * share * pack : (part + 1) * share * pack]
        if number + 1 not in (len(chunks) // 2 + 1, len(chunks)):
            continue
        ready = pl.ds(sent, number + 1 - sent)
        for step in range(1, n_sec):
            target = lax.rem(me + step, n_sec)
            slot = step - 1 + (n_sec - 1) * (number + 1 == len(chunks))
            outs.append(
                send(
                    sent_ref.at[target, ready], land_ref.at[me, ready],
                    out_send.at[slot], out_recv.at[slot], (target, brick),
                )
            )
        sent = number + 1
    land_ref[me] = sent_ref[me]
    shape = (share, snaps)
    pick = (
        lax.broadcasted_iota(jnp.int32, shape, 1)
        == lax.broadcasted_iota(jnp.int32, shape, 0) + me * share
    ).astype(F32)
    energy_ref[...] = exact(pick, covariance) / total_values

    for number in range(FIELDS // GROUP):
        for side in range(2):
            halo_copy(number, side).wait_send()
        for step in range(1, n_sec):
            part_copy(number, step, 0, held).wait_send()

    for copy in outs:
        copy.wait_recv()
    for copy in copies:
        copy.wait_send()


def widen(held, land_ref, energy_ref, out_ref, result_ref):
    n_sec, chunks, rows, width = land_ref.shape
    share = out_ref.shape[1]
    pack = rows // share
    for number in range(chunks):
        for source in range(n_sec):
            values = land_ref[source, number].astype(F32)
            for part in range(min(pack, FIELDS * held - number * pack)):
                field, piece = divmod(number * pack + part, held)
                column = (piece * n_sec + source) * width
                out_ref[field, :, column : column + width] = values[part * share : (part + 1) * share]
    result_ref[...] = energy_ref[...]


def per_device(n_sec, n_brick, velocity, filter_taps, start_vectors):
    _, snaps, rows, cells = velocity.shape
    reduced = cells // 4
    groups = rows // 4 + 2
    share = snaps // n_sec
    held = rows // 4 // n_sec
    slots = max(sum(radix for _, radix in radices(n_brick // 2)), 1)
    sets = FIELDS // GROUP
    count = n_sec * snaps
    batch = max(1, min(snaps, 256 // rows))
    total_values = n_sec * snaps * FIELDS * (rows // 2) * reduced * n_brick
    width = 2 * reduced
    dma = pltpu.SemaphoreType.DMA
    pack = max(1, 256 // count)
    chunks = -(-FIELDS * held // pack)
    landed, energies = pl.pallas_call(
        functools.partial(kernel, n_sec, n_brick, total_values),
        out_shape=(
            pltpu.VMEM((n_sec, chunks, pack * share, width), BF16),
            pltpu.VMEM((share, snaps), F32),
        ),
        in_specs=[
            pl.BlockSpec(memory_space=pl.ANY),
            pl.BlockSpec(memory_space=pltpu.SMEM),
            pl.BlockSpec(memory_space=pltpu.VMEM),
        ],
        out_specs=(
            pl.BlockSpec(memory_space=pltpu.VMEM),
            pl.BlockSpec(memory_space=pltpu.VMEM),
        ),
        scratch_shapes=[
            pltpu.VMEM((3, snaps, rows, cells), F32),
            pltpu.VMEM((3 * cells, reduced), BF16),
            pltpu.VMEM((2 * groups * batch, 3 * batch * rows), BF16),
            pltpu.VMEM((FIELDS, 2, snaps, width), F32),
            pltpu.VMEM((2, FIELDS, snaps, width), BF16),
            pltpu.VMEM((2, FIELDS, snaps, width), BF16),
            pltpu.VMEM((FIELDS, held, n_sec, snaps, width), BF16),
            pltpu.VMEM((FIELDS, held, n_sec, snaps, width), BF16),
            pltpu.VMEM((2, 2 * snaps, LANES), F32),
            pltpu.VMEM((2, count // 4, 2 * count), F32),
            pltpu.VMEM((count // 4, 2 * count), F32),
            pltpu.VMEM((slots, count // 4, 2 * count), F32),
            pltpu.VMEM((n_sec, count // 4, 2 * count), F32),
            pltpu.VMEM((2, count // 4, 2 * count), F32),
            pltpu.VMEM((n_sec, chunks, pack * share, width), BF16),
            dma((3,)),
            dma((sets, 2)),
            dma((sets, 2)),
            dma((sets, n_sec - 1)),
            dma((sets, n_sec - 1)),
            dma((2,)),
            dma((2,)),
            dma((slots,)),
            dma((slots,)),
            dma((n_sec - 1,)),
            dma((n_sec - 1,)),
            dma((2 * (n_sec - 1),)),
            dma((2 * (n_sec - 1),)),
        ],
        compiler_params=pltpu.CompilerParams(
            collective_id=0, has_side_effects=True, vmem_limit_bytes=60 * 1024 * 1024
        ),
    )(velocity, filter_taps, jnp.transpose(start_vectors, (0, 2, 1)))
    basis, energies = pl.pallas_call(
        functools.partial(widen, held),
        out_shape=(
            jax.ShapeDtypeStruct((FIELDS, share, rows // 2 * reduced), F32),
            jax.ShapeDtypeStruct((share, snaps), F32),
        ),
        in_specs=[pl.BlockSpec(memory_space=pltpu.VMEM)] * 2,
        out_specs=(pl.BlockSpec(memory_space=pltpu.VMEM),) * 2,
        compiler_params=pltpu.CompilerParams(vmem_limit_bytes=8 * 1024 * 1024),
    )(landed, energies)
    return jnp.transpose(basis, (1, 0, 2)), energies


def solution(mesh):
    in_specs = (P(None, "sec", "brick", None), P(), P())
    out_specs = (P("sec", None, "brick"), P("sec", None))
    return jax.shard_map(
        functools.partial(per_device, mesh.shape["sec"], mesh.shape["brick"]),
        mesh=mesh, in_specs=in_specs, out_specs=out_specs, check_vma=False,
    )
```

```python
import functools

import jax
import jax.numpy as jnp
from jax import lax
from jax.experimental import pallas as pl
from jax.experimental.pallas import tpu as pltpu
from jax.sharding import PartitionSpec as P

CY = 32
CZ = 24
NS_STEPS = 8
TAPS = 9
FIELDS = 9
GROUP = 3
LANES = 128
ROOT = 3.821640164404114
MESH = pl.DeviceIdType.MESH
F32 = jnp.float32
BF16 = jnp.bfloat16


def exact(a, b, dims=((1,), (0,))):
    return lax.dot_general(
        a, b, (dims, ((), ())), precision=lax.Precision.HIGHEST, preferred_element_type=F32
    )


def fast(a, b, dims=((1,), (0,))):
    return lax.dot_general(a, b, (dims, ((), ())), preferred_element_type=F32)


def split(value):
    high = value.astype(BF16)
    return high, (value - high.astype(F32)).astype(BF16)


def grid_of(shape, dim):
    return lax.broadcasted_iota(jnp.int32, shape, dim).astype(F32)


def eye_of(size):
    shape = (size, size)
    return (
        lax.broadcasted_iota(jnp.int32, shape, 0) == lax.broadcasted_iota(jnp.int32, shape, 1)
    ).astype(F32)


def trace_of(matrix):
    return jnp.sum(matrix * eye_of(matrix.shape[0]), keepdims=True)


def pick_taps(taps_ref, dim, offset):
    total = jnp.zeros_like(offset)
    for tap in range(TAPS):
        total = jnp.where(offset == float(tap), taps_ref[dim, tap], total)
    return total


def radices(size):
    result, stride = [], 1
    while size > 1:
        radix = 4 if size % 4 == 0 else 2
        result.append((stride, radix))
        stride, size = stride * radix, size // radix
    return result


def terms(value):
    first = value.astype(BF16)
    rest = value - first.astype(F32)
    second = rest.astype(BF16)
    last = rest - second.astype(F32)
    return first, second, last.astype(BF16), rest, last


def as_left(value, order):
    slot = lax.broadcasted_iota(jnp.int32, value.shape, 1) // order
    _, _, _, rest, last = terms(value)
    return jnp.where(slot < 3, value, jnp.where(slot < 5, rest, last)).astype(BF16)


def as_right(value):
    first, second, third, _, _ = terms(value)
    blocks = [first, second, third, first, second, first]
    blank = jnp.zeros_like(first)
    spare = LANES // value.shape[0] - len(blocks)
    return jnp.concatenate(blocks + [blank] * spare, axis=0)


def narrow(left, right):
    return fast(as_left(left, right.shape[0]), as_right(right))


def narrow_all(lefts, rights):
    if len(lefts) == 1:
        return [narrow(lefts[0], rights[0])]
    size = lefts[0].shape[0]
    joined = fast(
        jnp.concatenate([as_left(left, rights[0].shape[0]) for left in lefts], axis=0),
        jnp.concatenate([as_right(right) for right in rights], axis=1),
    )
    return [
        joined[place * size : (place + 1) * size, place * LANES : (place + 1) * LANES]
        for place in range(len(lefts))
    ]


def square_and_apply(values, products):
    order = values[0].shape[0]
    joined = narrow_all(
        [jnp.concatenate([v, z], axis=0) for v, z in zip(values, products)], values
    )
    return [j[:order] for j in joined], [z + 0.5 * j[order:] for j, z in zip(joined, products)]


def newton_factors(matrices, scales):
    order = matrices[0].shape[0]
    shape = (order, LANES)
    unit = (
        lax.broadcasted_iota(jnp.int32, shape, 0)
        == lax.rem(lax.broadcasted_iota(jnp.int32, shape, 1), order)
    ).astype(F32)
    gaps = [unit - m / s for m, s in zip(matrices, scales)]
    products = None
    left = NS_STEPS - 1
    while left > 0:
        if products is None:
            squares = narrow_all(gaps, gaps)
            products = [unit + 0.5 * v for v in gaps]
        else:
            squares, products = square_and_apply(gaps, products)
        if left < 3:
            gaps = narrow_all(squares, [0.75 * unit + 0.25 * v for v in gaps])
            left -= 1
        else:
            sums = [3.0 * v + w for w, v in zip(squares, gaps)]
            once = narrow_all(squares, [0.75 * unit + 0.25 * v for v in gaps])
            doubles = narrow_all(sums, sums)
            cross = narrow_all(squares, sums)
            powers, products = square_and_apply(once, products)
            heads = narrow_all(once, cross)
            tails = [
                (1.0 / 16) * narrow(c, d) + (3.0 + ROOT) * narrow(a, g) + (3.0 * ROOT) * a
                for a, c, d, g in zip(sums, cross, doubles, once)
            ]
            twice = narrow_all(powers, [0.75 * unit + 0.25 * g for g in once])
            highs = narrow_all(heads, tails)
            lows = [
                narrow(3.0 * g + p, p + (3.0 - ROOT) * g + ROOT * (ROOT - 3.0) * unit)
                for p, g in zip(powers, once)
            ]
            gaps = [v * (1.0 / 4096) for v in narrow_all(highs, lows)]
            products = narrow_all(products, [unit + 0.5 * w for w in twice])
            left -= 3
    factors = [unit + 0.5 * v for v in gaps]
    return [(z, e, 1.0 / jnp.sqrt(s)) for z, e, s in zip(products, factors, scales)]


def times_root(value, root):
    product, factor, scale = root
    return narrow(narrow(value, product) * scale, factor)


def root_times(value, root):
    product, factor, scale = root
    return narrow(factor, narrow(product, value) * scale)


def total_of(value, copies):
    total = jnp.sum(jnp.sum(value, axis=0, keepdims=True), axis=1, keepdims=True)
    return total * (1.0 / copies)


def merge_bases(grams, wides, start, start_t):
    size = grams[0].shape[0]
    copies = LANES // start_t.shape[0]
    traces = [trace_of(g) for g in grams]
    shares = [1.0 / t for t in traces]
    basis = [exact(g, start) * s for g, s in zip(grams, shares)]
    basis_t = [exact(start_t, w) * s for w, s in zip(wides, shares)]
    for repeat in range(2):
        metric = [exact(t[:, :size], b) for t, b in zip(basis_t, basis)]
        scales = [total_of(b * b, copies) for b in basis]
        image = [exact(g, b) * s for g, b, s in zip(grams, basis, shares)]
        image_t = [exact(t[:, :size], w) * s for t, w, s in zip(basis_t, wides, shares)]
        roots = newton_factors(metric, scales)
        if repeat == 0:
            basis = [times_root(b, r) for b, r in zip(image, roots)]
            basis_t = [root_times(t, r) for t, r in zip(image_t, roots)]
    basis = [times_root(b, r) for b, r in zip(basis, roots)]
    basis_t = [root_times(t, r) for t, r in zip(basis_t, roots)]
    image = [times_root(b, r) for b, r in zip(image, roots)]
    image_t = [root_times(t, r) for t, r in zip(image_t, roots)]
    metric = [exact(t[:, :size], b) for t, b in zip(basis_t, image)]
    scales = [total_of(q * b, copies) for q, b in zip(basis, image)]
    roots = newton_factors(metric, scales)
    project = [times_root(q, r) for q, r in zip(basis, roots)]
    project_t = [root_times(t, r) for t, r in zip(basis_t, roots)]
    image = [times_root(b, r) for b, r in zip(image, roots)]
    image_t = [root_times(t, r) for t, r in zip(image_t, roots)]
    metric = [exact(t[:, :size], b) for t, b in zip(image_t, image)]
    scales = [total_of(b * b, copies) for b in image]
    spread = [narrow(p, m) for p, m in zip(project, metric)]
    spread_t = [narrow(m, t) for t, m in zip(project_t, metric)]
    roots = newton_factors(metric, scales)
    coeffs = [times_root(p, r) for p, r in zip(spread, roots)]
    coeffs_t = [root_times(t, r) for t, r in zip(spread_t, roots)]
    covariance = [m * t for m, t in zip(metric, traces)]
    return coeffs, coeffs_t, covariance


def merge_tree(gram, starts, starts_t):
    order, size = starts_t[0].shape
    columns = [gram[:, part : part + size] for part in range(0, gram.shape[0], size)]
    grams = [column[part * size : (part + 1) * size] for part, column in enumerate(columns)]
    wides = [jnp.concatenate([g] * (LANES // size), axis=1) for g in grams]
    lower, lower_t, _ = merge_bases(grams, wides, starts[0], starts_t[0])
    images = [exact(column, basis) for column, basis in zip(columns, lower)]
    lane = lax.broadcasted_iota(jnp.int32, (order, LANES), 1)
    own = lax.rem(lane, size) < order
    rows = []
    for part, basis_t in enumerate(lower_t):
        left, right = [
            exact(basis_t[:, :size], image[part * size : (part + 1) * size]) for image in images
        ]
        rows.append(jnp.where(own, left, right))
    wide = jnp.concatenate(rows, axis=0)
    (_,), (coeffs_t,), (covariance,) = merge_bases([wide[:, :size]], [wide], starts[1], starts_t[1])
    joined = jnp.concatenate(
        [
            jnp.where(lax.rem(lane // size, len(lower_t)) == part, basis_t, 0.0)
            for part, basis_t in enumerate(lower_t)
        ],
        axis=0,
    )
    return exact(coeffs_t[:, :size], joined), covariance[:, :order]


def kernel(
    n_sec, n_brick, total_values,
    velocity_ref, taps_ref, start_ref,
    land_ref, energy_ref,
    field_ref, cross_ref, rows_ref, edge_ref, halo_out, halo_in, own_ref, all_ref,
    wide_ref, gram_out, core_in, z_in, sec_in, total_ref, sent_ref,
    load_sem, halo_send, halo_recv, part_send, part_recv,
    core_send, core_recv, z_send, z_recv, sec_send, sec_recv, out_send, out_recv,
):
    snaps, rows = velocity_ref.shape[1], velocity_ref.shape[2]
    cells = velocity_ref.shape[3]
    reduced = cells // 4
    groups = rows // 4 + 2
    batch = rows_ref.shape[0] // (2 * groups)
    share = snaps // n_sec
    held = own_ref.shape[1]
    me = lax.axis_index("sec")
    brick = lax.axis_index("brick")
    low = lax.rem(brick + n_brick - 1, n_brick)
    high = lax.rem(brick + 1, n_brick)
    core = lax.rem(brick, 2)
    partner = brick + 1 - 2 * core
    stages = []
    for stride, radix in radices(n_brick // 2):
        digit = lax.rem(brick // (2 * stride), radix)
        peers = [
            brick + 2 * stride * (lax.rem(digit + step, radix) - digit) for step in range(1, radix)
        ]
        stages.append((digit, peers))
    near = [low, high] + [peer for _, peers in stages for peer in peers]

    loads = []
    for number in range(3):
        copy = pltpu.make_async_copy(
            velocity_ref.at[number], field_ref.at[number], load_sem.at[number]
        )
        copy.start()
        loads.append(copy)

    barrier = pltpu.get_barrier_semaphore()
    for target in near:
        pl.semaphore_signal(barrier, inc=1, device_id=(me, target), device_id_type=MESH)
    for step in range(1, n_sec):
        pl.semaphore_signal(
            barrier, inc=1, device_id=(lax.rem(me + step, n_sec), brick), device_id_type=MESH
        )

    for level in range(2):
        wide_ref[level] = jnp.concatenate([start_ref[level].T] * (LANES // snaps), axis=1)

    shape = (CY, reduced)
    y, point = grid_of(shape, 0), grid_of(shape, 1)
    j = jnp.floor((point + 0.5) * (2.0 / CZ))
    off_y = y - 2.0 * j + 4.0
    off_y = jnp.where(off_y < 0.0, off_y + CY, off_y)
    off_y = jnp.where(off_y >= CY, off_y - CY, off_y)
    along_y = pick_taps(taps_ref, 1, off_y)
    shape = (CZ, reduced)
    z, point = grid_of(shape, 0), grid_of(shape, 1)
    k = point - jnp.floor((point + 0.5) * (2.0 / CZ)) * (CZ // 2)
    off_z = z - 2.0 * k + 4.0
    off_z = jnp.where(off_z < 0.0, off_z + CZ, off_z)
    off_z = jnp.where(off_z >= CZ, off_z - CZ, off_z)
    along_z = pick_taps(taps_ref, 2, off_z)
    for pair in range(0, CY, 2):
        upper, lower = split(
            jnp.concatenate([along_y[row : row + 1] * along_z for row in (pair, pair + 1)], axis=0)
        )
        place = pair * CZ
        cross_ref[place : place + 2 * CZ, :] = upper
        cross_ref[cells + place : cells + place + 2 * CZ, :] = upper
        cross_ref[2 * cells + place : 2 * cells + place + 2 * CZ, :] = lower

    shape = (2 * groups * batch, batch * rows)
    target, source = grid_of(shape, 0), grid_of(shape, 1)
    parity = (target >= groups * batch).astype(F32)
    rest = target - parity * (groups * batch)
    pair = jnp.floor((rest + 0.5) * (1.0 / batch))
    snap = rest - pair * batch
    snap_in = jnp.floor((source + 0.5) * (1.0 / rows))
    offset = (source - snap_in * rows) - 2.0 * (2.0 * pair + parity - 2.0) + 4.0
    offset = jnp.where(snap == snap_in, offset, -1.0)
    upper, lower = split(pick_taps(taps_ref, 0, offset))
    width = batch * rows
    rows_ref[:, 0:width] = upper
    rows_ref[:, width : 2 * width] = upper
    rows_ref[:, 2 * width :] = lower

    def halo_copy(number, side):
        fields = pl.ds(number * GROUP, GROUP)
        return pltpu.make_async_remote_copy(
            src_ref=halo_out.at[side, fields],
            dst_ref=halo_in.at[1 - side, fields],
            send_sem=halo_send.at[number, side],
            recv_sem=halo_recv.at[number, 1 - side],
            device_id=(me, low if side == 0 else high),
            device_id_type=MESH,
        )

    def part_copy(number, step, first, size):
        fields = pl.ds(number * GROUP, GROUP)
        target = lax.rem(me + step, n_sec)
        return pltpu.make_async_remote_copy(
            src_ref=own_ref.at[fields, pl.ds(first, size), target],
            dst_ref=all_ref.at[fields, pl.ds(first, size), me],
            send_sem=part_send.at[number, step - 1],
            recv_sem=part_recv.at[number, step - 1],
            device_id=(target, brick),
            device_id_type=MESH,
        )

    def is_first(step):
        return (lax.rem(me + step, n_sec) == 0).astype(jnp.int32)

    def filtered(number, values, first=False):
        fields = [number * GROUP + place for place in range(GROUP)]
        inner = []
        for place in range(GROUP):
            upper, lower = split(values(place).reshape(snaps * rows, cells))
            inner.append(fast(jnp.concatenate([upper, lower, upper], axis=1), cross_ref[...]))
        half = groups * batch
        results = []
        for value in inner:
            upper, lower = split(value)
            blocks = []
            for start in range(0, snaps * rows, width):
                high_part, low_part = upper[start : start + width], lower[start : start + width]
                outer = fast(rows_ref[...], jnp.concatenate([high_part, low_part, high_part], axis=0))
                joined = jnp.concatenate([outer[:half], outer[half:]], axis=1)
                blocks.append(joined.reshape(groups, batch, 2 * reduced))
            results.append(jnp.concatenate(blocks, axis=1))
        if first:
            pl.semaphore_wait(barrier, len(near) + n_sec - 1)
        for field, joined in zip(fields, results):
            halo_out[0, field] = joined[0].astype(BF16)
            halo_out[1, field] = joined[groups - 1].astype(BF16)
            edge_ref[field, 0] = joined[1]
            edge_ref[field, 1] = joined[groups - 2]
            for group in range(1, groups - 3):
                own_ref[field, group // n_sec, group % n_sec] = joined[group + 1].astype(BF16)
        halo_copy(number, 0).start()
        halo_copy(number, 1).start()
        if held > 1:
            for step in range(1, n_sec):
                part_copy(number, step, is_first(step), held - 1).start()

    def finish(number):
        fields = [number * GROUP + place for place in range(GROUP)]
        halo_copy(number, 1).wait_recv()
        halo_copy(number, 0).wait_recv()
        for field in fields:
            own_ref[field, 0, 0] = (edge_ref[field, 0] + halo_in[0, field].astype(F32)).astype(BF16)
            own_ref[field, held - 1, n_sec - 1] = (
                edge_ref[field, 1] + halo_in[1, field].astype(F32)
            ).astype(BF16)
        for step in range(1, n_sec):
            part_copy(number, step, (held - 1) * (1 - is_first(step)), 1).start()
        for field in fields:
            for piece in range(held):
                all_ref[field, piece, me] = own_ref[field, piece, me]


    def source(number):
        one = number // 3 + number // 5
        two = number - 3 * one + one * (one - 1) // 2 + one
        return field_ref[one] * field_ref[two]

    def component(number):
        loads[number].wait()
        return field_ref[number]

    filtered(0, component, True)

    def step_on(number, carry):
        filtered(number, lambda place: source((number - 1) * GROUP + place))
        finish(number - 1)
        return carry

    lax.fori_loop(1, FIELDS // GROUP, step_on, 0)
    finish(FIELDS // GROUP - 1)

    count = n_sec * snaps
    gram = jnp.zeros((count, count), F32)
    for field in range(FIELDS):
        if field % GROUP == 0:
            for step in range(1, n_sec):
                part_copy(field // GROUP, step, 0, held).wait_recv()
        for piece in range(held):
            block = all_ref[field, piece].reshape(count, 2 * reduced)
            gram = gram + fast(block, block, ((1,), (1,)))

    half = count // 4
    gram_out[0] = jnp.concatenate([gram[:half], gram[half : 2 * half]], axis=1)
    gram_out[1] = jnp.concatenate([gram[2 * half : 3 * half], gram[3 * half :]], axis=1)
    copies = []

    def send(source, landing, sender, receiver, device):
        copy = pltpu.make_async_remote_copy(
            src_ref=source, dst_ref=landing, send_sem=sender, recv_sem=receiver,
            device_id=device, device_id_type=MESH,
        )
        copy.start()
        copies.append(copy)
        return copy

    send(
        gram_out.at[1 - core], core_in, core_send.at[0], core_recv.at[0], (me, partner)
    ).wait_recv()
    total = gram_out[core] + core_in[...]
    offset = 0
    for digit, peers in stages:
        z_in[offset + digit] = total
        landed = [
            send(
                z_in.at[offset + digit], z_in.at[offset + digit],
                z_send.at[offset + step], z_recv.at[offset + step], (me, peer),
            )
            for step, peer in enumerate(peers)
        ]
        for copy in landed:
            copy.wait_recv()
        total = z_in[offset]
        for slot in range(1, len(peers) + 1):
            total = total + z_in[offset + slot]
        offset += len(peers) + 1
    sec_in[me] = total
    landed = [
        send(
            sec_in.at[me], sec_in.at[me], sec_send.at[step - 1], sec_recv.at[step - 1],
            (lax.rem(me + step, n_sec), brick),
        )
        for step in range(1, n_sec)
    ]
    for copy in landed:
        copy.wait_recv()
    total = sec_in[0]
    for slot in range(1, n_sec):
        total = total + sec_in[slot]
    total_ref[core] = total
    send(
        total_ref.at[core], total_ref.at[core], core_send.at[1], core_recv.at[1], (me, partner)
    ).wait_recv()
    first, second = total_ref[0], total_ref[1]
    gram = jnp.concatenate(
        [first[:, :count], first[:, count:], second[:, :count], second[:, count:]], axis=0
    )

    weights, covariance = merge_tree(
        gram, [wide_ref[0], wide_ref[1]], [start_ref[0], start_ref[1]]
    )
    pack = sent_ref.shape[2] // share
    weights = jnp.concatenate([weights] * (pack * count // LANES), axis=1)
    weights = jnp.concatenate(
        [weights[part : part + share] for part in range(0, snaps, share) for _ in range(pack)], axis=0
    )
    row = lax.broadcasted_iota(jnp.int32, weights.shape, 0)
    lane = lax.broadcasted_iota(jnp.int32, weights.shape, 1)
    weights = jnp.where(lax.rem(row // share, pack) == lane // count, weights, 0.0)
    upper, lower = split(weights)
    weights = jnp.concatenate([upper, lower], axis=0)
    shape = (share, snaps)
    pick = (
        lax.broadcasted_iota(jnp.int32, shape, 1)
        == lax.broadcasted_iota(jnp.int32, shape, 0) + me * share
    ).astype(F32)
    energy_ref[...] = exact(pick, covariance) / total_values

    outs = []
    places = [(field, piece) for field in range(FIELDS) for piece in range(held)]
    chunks = [places[first : first + pack] for first in range(0, len(places), pack)]
    sent = 0
    for number, chunk in enumerate(chunks):
        blocks = jnp.concatenate(
            [all_ref[field, piece].reshape(count, 2 * reduced) for field, piece in chunk], axis=0
        )
        values = fast(weights[:, : len(chunk) * count], blocks)
        values = (values[: snaps * pack] + values[snaps * pack :]).astype(BF16)
        for part in range(n_sec):
            sent_ref[part, number] = values[part * share * pack : (part + 1) * share * pack]
        if number + 1 not in (len(chunks) // 2, len(chunks)):
            continue
        ready = pl.ds(sent, number + 1 - sent)
        for step in range(1, n_sec):
            target = lax.rem(me + step, n_sec)
            slot = step - 1 + (n_sec - 1) * (number + 1 == len(chunks))
            outs.append(
                send(
                    sent_ref.at[target, ready], land_ref.at[me, ready],
                    out_send.at[slot], out_recv.at[slot], (target, brick),
                )
            )
        sent = number + 1
    land_ref[me] = sent_ref[me]

    for number in range(FIELDS // GROUP):
        for side in range(2):
            halo_copy(number, side).wait_send()
        for step in range(1, n_sec):
            part_copy(number, step, 0, held).wait_send()

    for copy in outs:
        copy.wait_recv()
    for copy in copies:
        copy.wait_send()


def widen(held, land_ref, energy_ref, out_ref, result_ref):
    n_sec, chunks, rows, width = land_ref.shape
    share = out_ref.shape[1]
    pack = rows // share
    for number in range(chunks):
        for source in range(n_sec):
            values = land_ref[source, number].astype(F32)
            for part in range(min(pack, FIELDS * held - number * pack)):
                field, piece = divmod(number * pack + part, held)
                column = (piece * n_sec + source) * width
                out_ref[field, :, column : column + width] = values[part * share : (part + 1) * share]
    result_ref[...] = energy_ref[...]


def per_device(n_sec, n_brick, velocity, filter_taps, start_vectors):
    _, snaps, rows, cells = velocity.shape
    reduced = cells // 4
    groups = rows // 4 + 2
    share = snaps // n_sec
    held = rows // 4 // n_sec
    slots = max(sum(radix for _, radix in radices(n_brick // 2)), 1)
    sets = FIELDS // GROUP
    count = n_sec * snaps
    batch = max(1, min(snaps, 256 // rows))
    total_values = n_sec * snaps * FIELDS * (rows // 2) * reduced * n_brick
    width = 2 * reduced
    dma = pltpu.SemaphoreType.DMA
    pack = max(1, 256 // count)
    chunks = -(-FIELDS * held // pack)
    landed, energies = pl.pallas_call(
        functools.partial(kernel, n_sec, n_brick, total_values),
        out_shape=(
            pltpu.VMEM((n_sec, chunks, pack * share, width), BF16),
            pltpu.VMEM((share, snaps), F32),
        ),
        in_specs=[
            pl.BlockSpec(memory_space=pl.ANY),
            pl.BlockSpec(memory_space=pltpu.SMEM),
            pl.BlockSpec(memory_space=pltpu.VMEM),
        ],
        out_specs=(
            pl.BlockSpec(memory_space=pltpu.VMEM),
            pl.BlockSpec(memory_space=pltpu.VMEM),
        ),
        scratch_shapes=[
            pltpu.VMEM((3, snaps, rows, cells), F32),
            pltpu.VMEM((3 * cells, reduced), BF16),
            pltpu.VMEM((2 * groups * batch, 3 * batch * rows), BF16),
            pltpu.VMEM((FIELDS, 2, snaps, width), F32),
            pltpu.VMEM((2, FIELDS, snaps, width), BF16),
            pltpu.VMEM((2, FIELDS, snaps, width), BF16),
            pltpu.VMEM((FIELDS, held, n_sec, snaps, width), BF16),
            pltpu.VMEM((FIELDS, held, n_sec, snaps, width), BF16),
            pltpu.VMEM((2, 2 * snaps, LANES), F32),
            pltpu.VMEM((2, count // 4, 2 * count), F32),
            pltpu.VMEM((count // 4, 2 * count), F32),
            pltpu.VMEM((slots, count // 4, 2 * count), F32),
            pltpu.VMEM((n_sec, count // 4, 2 * count), F32),
            pltpu.VMEM((2, count // 4, 2 * count), F32),
            pltpu.VMEM((n_sec, chunks, pack * share, width), BF16),
            dma((3,)),
            dma((sets, 2)),
            dma((sets, 2)),
            dma((sets, n_sec - 1)),
            dma((sets, n_sec - 1)),
            dma((2,)),
            dma((2,)),
            dma((slots,)),
            dma((slots,)),
            dma((n_sec - 1,)),
            dma((n_sec - 1,)),
            dma((2 * (n_sec - 1),)),
            dma((2 * (n_sec - 1),)),
        ],
        compiler_params=pltpu.CompilerParams(
            collective_id=0, has_side_effects=True, vmem_limit_bytes=60 * 1024 * 1024
        ),
    )(velocity, filter_taps, jnp.transpose(start_vectors, (0, 2, 1)))
    basis, energies = pl.pallas_call(
        functools.partial(widen, held),
        out_shape=(
            jax.ShapeDtypeStruct((FIELDS, share, rows // 2 * reduced), F32),
            jax.ShapeDtypeStruct((share, snaps), F32),
        ),
        in_specs=[pl.BlockSpec(memory_space=pltpu.VMEM)] * 2,
        out_specs=(pl.BlockSpec(memory_space=pltpu.VMEM),) * 2,
        compiler_params=pltpu.CompilerParams(vmem_limit_bytes=8 * 1024 * 1024),
    )(landed, energies)
    return jnp.transpose(basis, (1, 0, 2)), energies


def solution(mesh):
    in_specs = (P(None, "sec", "brick", None), P(), P())
    out_specs = (P("sec", None, "brick"), P("sec", None))
    return jax.shard_map(
        functools.partial(per_device, mesh.shape["sec"], mesh.shape["brick"]),
        mesh=mesh, in_specs=in_specs, out_specs=out_specs, check_vma=False,
    )
```
